256 devices in a mesh: grp: 16 (over z_lo, y), dev: 16 (over x, z_hi, core).
Axes of the slice: x: 4, y: 4, z: 8 (z_hi: 2, z_lo: 4; z = z_hi * 4 + z_lo), core: 2. Of those that a mesh axis runs over, the one named last changes fastest.
Arguments:
- right_side: float32 [16, 16, 3, 4096], P('grp', 'dev'), may hold values from -15 to 15
- elem_nodes: int32 [16, 16, 27, 512], P('grp', 'dev'), may hold values from 0 to 4095, as said below
- elem_coef: float32 [16, 16, 512], P('grp', 'dev'), may hold values from 0.2 to 5
- node_mass: float32 [16, 16, 3, 4096], P('grp', 'dev'), may hold values from 0.5 to 4
- face_slots: int32 [16, 16, 4, 512], P('grp', 'dev'), may hold values from 0 to 4096, as said below
- coarse_nodes: int32 [16, 16, 4, 4096], P('grp', 'dev'), may hold values from 0 to 1535, as said below
- coarse_weights: float32 [16, 16, 4, 4096], P('grp', 'dev'), may hold values from 0.1 to 0.6
- elem_matrix: float32 [81, 81], replicated, may hold values from -1 to 2, as said below
- chol_inverse: float32 [4608, 4608], P('dev'), may hold values from -1 to 1, as said below
Outputs:
- preconditioned: float32 [16, 16, 3, 4096], P('grp', 'dev')
The draws below stay inside these ranges and needn't reach their ends.
Inputs may be any that keep to these rules, and one draw needn't show every extreme that they name: `elem_nodes`: the 27 entries of one element are distinct. `face_slots`: an entry 4096 is padding; the other entries of one subdomain are distinct. Slot p of a face and slot p of the neighbour's face back name the same shared node: both are padding or neither. Live slots come first in a face; faces with no neighbour subdomain are all padding; some face has all 512 slots live. `coarse_nodes`: the entries of subdomain (g, d) lie in the 64 coarse nodes from ((16 * g + d) * 1536) // 256 on, counted modulo 1536. `elem_matrix`: Symmetric; each diagonal entry is positive and exceeds the sum of the magnitudes of the other entries of its row. `chol_inverse`: lower triangular with a positive diagonal.
All inputs are finite; a program needn't handle non-finite values.
Results may differ from the reference program's by a relative error of at most 0.0001.
Values sent between devices are 32-bit elements; how exact they have to be, the bound alone decides.
A program may use at most 128 MiB of HBM per device.

```python
import math
from functools import partial
import jax
import jax.numpy as jnp
from jax import lax

ELEM = 512
FACE = 512
CN = 1536
PRE = 2
POST = 2
NL = 4096
NC = 4608
N_GRP = 16
N_DEV = 16


def draw_elem_nodes(key, part):
    key_base, key_step = jax.random.split(jax.random.fold_in(key, 3))
    first = jax.random.randint(key_base, (N_GRP, N_DEV, 1, ELEM), 0, NL)
    stride = jax.random.randint(key_step, (N_GRP, N_DEV, 1, ELEM), 1, NL // 32 + 1)
    offset = jnp.arange(27, dtype=jnp.int32)[None, None, :, None]
    return ((first + offset * stride) % NL).astype(jnp.int32)


def draw_face_slots(key, part):
    key_perm, key_grp, key_dev = jax.random.split(jax.random.fold_in(key, 11), 3)
    subkeys = jax.random.split(key_perm, N_GRP * N_DEV)

    def pick_slots(subkey):
        return jax.random.permutation(subkey, NL)[:4 * FACE]
    chosen = jax.vmap(pick_slots)(subkeys).reshape(N_GRP, N_DEV, 4, FACE).astype(jnp.int32)
    grp_live = jax.random.randint(key_grp, (N_GRP + 1, N_DEV), FACE // 2, FACE + 1)
    grp_live = grp_live.at[1, 0].set(FACE)
    grp_row = jnp.arange(N_GRP + 1)[:, None]
    grp_live = jnp.where((grp_row == 0) | (grp_row == N_GRP), 0, grp_live)
    dev_live = jax.random.randint(key_dev, (N_GRP, N_DEV + 1), FACE // 2, FACE + 1)
    dev_col = jnp.arange(N_DEV + 1)[None, :]
    dev_live = jnp.where((dev_col == 0) | (dev_col == N_DEV), 0, dev_live)
    counts = jnp.stack([grp_live[:-1], grp_live[1:], dev_live[:, :-1], dev_live[:, 1:]], axis=2)
    slot_number = jnp.arange(FACE)[None, None, None, :]
    return jnp.where(slot_number < counts[..., None], chosen, NL).astype(jnp.int32)


def draw_coarse_nodes(key, part):
    device = jnp.arange(N_GRP * N_DEV, dtype=jnp.int32).reshape(N_GRP, N_DEV, 1, 1)
    home = device * CN // (N_GRP * N_DEV)
    spread = jax.random.randint(jax.random.fold_in(key, 23), (N_GRP, N_DEV, 4, NL), 0, 64)
    return ((home + spread) % CN).astype(jnp.int32)


def draw_elem_matrix(key, part):
    key_off, key_diag = jax.random.split(jax.random.fold_in(key, 5))
    raw = 0.012 * jax.random.normal(key_off, (81, 81), jnp.float32)
    upper = jnp.triu(raw, 1)
    offdiag = upper + upper.T
    dominant = 1.25 * jnp.sum(jnp.abs(offdiag), axis=1) + jax.random.uniform(key_diag, (81,), jnp.float32, 0.1, 0.4)
    return offdiag + jnp.diag(dominant)


def draw_chol_inverse(key, part):
    key_off, key_diag = jax.random.split(jax.random.fold_in(key, 7))
    raw = 0.06 * jax.random.normal(key_off, (NC, NC), jnp.float32) / jnp.sqrt(1.0 * NC)
    diagonal = jax.random.uniform(key_diag, (NC,), jnp.float32, 0.1, 0.2)
    return jnp.tril(raw, -1) + jnp.diag(diagonal)


def levels(stream_key, shape, cuts, least, largest):
    factor_of = 1.0
    for position, parts in cuts:
        steps = jax.random.uniform(jax.random.fold_in(jax.random.fold_in(stream_key, 6), position), (parts,), jnp.float32, least / len(cuts), largest / len(cuts))
        factor_of = factor_of * jnp.repeat(jnp.exp(steps), shape[position] // parts).reshape((-1,) + (1,) * (len(shape) - 1 - position))
    return factor_of


def bell_draw(key, extent, scale, reach, cuts=(), kind=jnp.bfloat16):
    array = jax.random.normal(key, extent, jnp.float32) * scale
    if len(cuts) > 0:
        array = levels(key, extent, cuts, -0.22, 0.18) * array
    return jnp.clip(array, min=-reach, max=reach).astype(kind)


def setup_inputs(seed: int = 0) -> dict:
    seeds = jax.random.split(jax.random.key(seed), 10)
    return {
        "right_side": bell_draw(seeds[0], (N_GRP, N_DEV, 3, NL), 3.0, 15.0, ((0, 16), (1, 16)), jnp.float32),
        "elem_nodes": draw_elem_nodes(jax.random.fold_in(seeds[9], 71), 0),
        "elem_coef": jnp.clip(jnp.exp(math.log(5.0) - 3.218876 * jax.random.uniform(seeds[2], (N_GRP, N_DEV, ELEM), jnp.float32) ** levels(seeds[2], (N_GRP, N_DEV, ELEM), ((0, 16), (1, 16)), -0.2, 0.2)), 0.2, 5.0),
        "node_mass": jnp.clip(jnp.exp(math.log(4.0) - 2.0794415 * jax.random.uniform(seeds[3], (N_GRP, N_DEV, 3, NL), jnp.float32) ** levels(seeds[3], (N_GRP, N_DEV, 3, NL), ((0, 16), (1, 16)), -0.2, 0.2)), 0.5, 4.0),
        "face_slots": draw_face_slots(jax.random.fold_in(seeds[9], 71), 0),
        "coarse_nodes": draw_coarse_nodes(jax.random.fold_in(seeds[9], 71), 0),
        "coarse_weights": jnp.clip(0.1 + 0.5 * jax.random.uniform(seeds[6], (N_GRP, N_DEV, 4, NL), jnp.float32) ** levels(seeds[6], (N_GRP, N_DEV, 4, NL), ((0, 16), (1, 16)), -0.2, 0.2), 0.1, 0.6),
        "elem_matrix": draw_elem_matrix(jax.random.fold_in(seeds[9], 71), 0),
        "chol_inverse": draw_chol_inverse(jax.random.fold_in(seeds[9], 71), 0),
    }


DAMPING = 0.6
PRECISE = lax.Precision.HIGHEST


def over_devices(function, arrays):
    def mapped(row_arrays):
        return jax.vmap(function)(*row_arrays)
    return lax.map(mapped, arrays)


def element_apply(matrix, field, node_index, elem_scale, mass_here):
    elem_count = node_index.shape[1]
    gathered = field[:, node_index].reshape(81, elem_count)
    product = jnp.dot(matrix, gathered, precision=PRECISE) * elem_scale[None, :]
    summed = jnp.zeros_like(field).at[:, node_index].add(product.reshape(3, 27, elem_count))
    return summed + mass_here * field


def local_diagonal(main_diag, node_index, elem_scale, mass_here):
    summed = jnp.zeros_like(mass_here).at[:, node_index].add(main_diag[:, :, None] * elem_scale[None, None, :])
    return summed + mass_here


def face_values(field, face_index):
    return field.at[:, face_index].get(mode="fill", fill_value=0.0)


def add_received(field, face_index, received):
    return field.at[:, face_index].add(received, mode="drop")


def assemble(field, face_slots):
    outgoing = over_devices(face_values, (field, face_slots))
    zero_grp = jnp.zeros_like(outgoing[:1, :, :, 0])
    from_below = jnp.concatenate([zero_grp, outgoing[:-1, :, :, 1]], axis=0)
    from_above = jnp.concatenate([outgoing[1:, :, :, 0], zero_grp], axis=0)
    zero_dev = jnp.zeros_like(outgoing[:, :1, :, 0])
    from_left = jnp.concatenate([zero_dev, outgoing[:, :-1, :, 3]], axis=1)
    from_right = jnp.concatenate([outgoing[:, 1:, :, 2], zero_dev], axis=1)
    received = jnp.stack([from_below, from_above, from_left, from_right], axis=3)
    return over_devices(add_received, (field, face_slots, received))


def restrict(coarse_width, field, coarse_index, weights):
    values = weights[None] * field[:, None, :]
    return jnp.zeros((3, coarse_width), field.dtype).at[:, coarse_index].add(values).reshape(3 * coarse_width)


def prolong(coarse, coarse_index, weights):
    coarse_table = coarse.reshape(3, coarse.shape[0] // 3)
    return jnp.sum(weights[None] * coarse_table[:, coarse_index], axis=1)


def reference(right_side, elem_nodes, elem_coef, node_mass, face_slots, coarse_nodes, coarse_weights, elem_matrix, chol_inverse):
    main_diag = jnp.diagonal(elem_matrix).reshape(3, 27)

    def operate(field):
        local = over_devices(partial(element_apply, elem_matrix), (field, elem_nodes, elem_coef, node_mass))
        return assemble(local, face_slots)

    local_diag = over_devices(partial(local_diagonal, main_diag), (elem_nodes, elem_coef, node_mass))
    diag_total = assemble(local_diag, face_slots)
    iterate = DAMPING * right_side / diag_total
    for sweep_index in range(PRE - 1):
        iterate = iterate + DAMPING * (right_side - operate(iterate)) / diag_total
    residual = right_side - operate(iterate)
    pieces = over_devices(partial(restrict, CN), (residual, coarse_nodes, coarse_weights))
    coarse_rhs = jnp.sum(pieces, axis=(0, 1))
    halfway = jnp.dot(chol_inverse, coarse_rhs, precision=PRECISE)
    correction = jnp.dot(halfway, chol_inverse, precision=PRECISE)
    iterate = iterate + over_devices(partial(prolong, correction), (coarse_nodes, coarse_weights))
    for sweep_index in range(POST):
        iterate = iterate + DAMPING * (right_side - operate(iterate)) / diag_total
    return iterate
```

```python
import jax
import jax.numpy as jnp
from jax import lax
from jax.experimental import pallas as pl
from jax.experimental.pallas import tpu as pltpu
from jax.sharding import PartitionSpec as P

DAMPING = 0.6
MESH = pl.DeviceIdType.MESH
BF16 = jnp.bfloat16
F32 = jnp.float32
I32 = jnp.int32
NT = (((1,), (1,)), ((), ()))
NN = (((1,), (0,)), ((), ()))

ROWS = 32
NODES_PER = 27
ELEM = 512
CN = 1536
WIN = 64
RB = 288


def dot(a, b, dims):
    return lax.dot_general(a, b, dims, preferred_element_type=F32)


def dot_exact(a, b, dims):
    return lax.dot_general(
        a, b, dims, precision=lax.Precision.HIGHEST, preferred_element_type=F32
    )


def split(x):
    high = x.astype(BF16)
    low = (x - high.astype(F32)).astype(BF16)
    return high, low


def lane_gather(row, lanes):
    return jnp.take_along_axis(row, lanes, axis=1, mode="promise_in_bounds")


def pick(load_row, rows, hi, lo, fields):
    got = [jnp.zeros(hi.shape, F32) for _ in range(fields)]
    for r in range(rows):
        here = hi == r
        for c in range(fields):
            row = jnp.broadcast_to(load_row(c, r), hi.shape)
            got[c] = jnp.where(here, lane_gather(row, lo), got[c])
    return got


def kernel(
    n_grp, n_dev,
    rhs_ref, nodes_ref, coef_ref, mass_ref, face_ref, cn_ref, cw_ref, em_ref, chol_ref,
    out_ref,
    z_t, w_t, rhs_t, mass_t, dinv_t, hi_i, lo_i, gath, p_hi, p_lo, m_hl, bt, oh,
    f_hi, f_lo, v_hi, v_lo, pwh, pwl, flat,
    send, recv, s1_send, s1_recv, s2_send, s2_recv, s3_send, s3_recv, lblk,
    send_sem, recv_sem, s1_ss, s1_rs, s2_ss, s2_rs, s3_ss, s3_rs, l_sem,
):
    g = lax.axis_index("grp")
    d = lax.axis_index("dev")

    block0 = (3 * g) // 4
    block1 = lax.rem(block0 + 1, CN // 128)
    l_copies = []
    for c in range(3):
        for b, block in enumerate((block0, block1)):
            at = pl.multiple_of(CN * c + 128 * block, 128)
            copy = pltpu.make_async_copy(
                chol_ref.at[:, pl.ds(at, 128)], lblk.at[2 * c + b], l_sem.at[2 * c + b]
            )
            copy.start()
            l_copies.append(copy)

    barrier = pltpu.get_barrier_semaphore()
    for k in range(1, n_dev):
        pl.semaphore_signal(
            barrier, inc=1, device_id=(g, lax.rem(d + k, n_dev)), device_id_type=MESH
        )
    for k in range(1, n_grp):
        pl.semaphore_signal(
            barrier, inc=1, device_id=(lax.rem(g + k, n_grp), d), device_id_type=MESH
        )

    for c in range(3):
        for r in range(ROWS):
            rhs_t[c * ROWS + r : c * ROWS + r + 1, :] = rhs_ref[c : c + 1, 128 * r : 128 * r + 128]
            mass_t[c * ROWS + r : c * ROWS + r + 1, :] = mass_ref[c : c + 1, 128 * r : 128 * r + 128]
    for f in range(4):
        for r in range(4):
            face = face_ref[f : f + 1, 128 * r : 128 * r + 128]
            f_hi[4 * f + r : 4 * f + r + 1, :] = face >> 7
            f_lo[4 * f + r : 4 * f + r + 1, :] = face & 127

    hi_i[...] = jnp.zeros((32, ELEM), I32)
    lo_i[...] = jnp.zeros((32, ELEM), I32)
    hi_i[0:NODES_PER, :] = nodes_ref[...] >> 7
    lo_i[0:NODES_PER, :] = nodes_ref[...] & 127

    def one_hot(index_row, count):
        at = jnp.broadcast_to(index_row, (count, index_row.shape[1]))
        number = lax.broadcasted_iota(I32, at.shape, 0)
        return jnp.where(at == number, 1.0, 0.0).astype(BF16)

    def make_one_hot(i, carry):
        oh[i] = one_hot(hi_i[pl.ds(i, 1), :], ROWS)
        bt[i] = one_hot(lo_i[pl.ds(i, 1), :], 128)
        return carry

    lax.fori_loop(0, NODES_PER, make_one_hot, 0)

    row_of = lax.broadcasted_iota(I32, (96, 81), 0)
    col_of = lax.broadcasted_iota(I32, (96, 81), 1)
    place = (col_of == 27 * (row_of // 32) + row_of % 32) & (row_of % 32 < 27)
    place = jnp.where(place, 1.0, 0.0)
    matrix = dot_exact(dot_exact(place, em_ref[...], NN), place, NT)
    mh, ml = split(matrix)
    m_hl[0:96, :] = mh
    m_hl[96:192, :] = ml
    eye = lax.broadcasted_iota(I32, (96, 96), 0) == lax.broadcasted_iota(I32, (96, 96), 1)
    main_diag = jnp.sum(jnp.where(eye, matrix, 0.0), axis=1, keepdims=True)
    coef = coef_ref[...]

    def put_product(product):
        high = product.astype(BF16).astype(F32)
        p_hi[...] = high
        p_lo[...] = product - high

    def scatter():
        def body(i, acc):
            hot = oh[i]
            blocks = []
            for part in (p_hi, p_lo):
                for c in range(3):
                    row = part[pl.ds(c * 32 + i, 1), :]
                    value = jnp.broadcast_to(row, (ROWS, ELEM)).astype(BF16)
                    blocks.append(value * hot)
            return acc + dot(jnp.concatenate(blocks, axis=0), bt[i], NT)

        acc = lax.fori_loop(0, NODES_PER, body, jnp.zeros((192, 128), F32))
        return acc[0:96] + acc[96:192]

    acc = jnp.zeros((64, 128), F32)
    for f in range(4):
        face = face_ref[f : f + 1, :]
        hot = one_hot(face >> 7, ROWS)
        slot = lax.broadcasted_iota(I32, (ROWS, ELEM), 1) + (512 * f + 1)
        a = jnp.concatenate(
            [(slot >> 6).astype(F32).astype(BF16) * hot, (slot & 63).astype(F32).astype(BF16) * hot],
            axis=0,
        )
        acc = acc + dot(a, one_hot(face & 127, 128), NT)
    inverse = (64.0 * acc[0:32] + acc[32:64]).astype(I32) - 1
    v_hi[...] = inverse >> 7
    v_lo[...] = inverse & 127

    put_product(main_diag * coef)
    w_t[...] = mass_t[...] + scatter()

    pl.semaphore_wait(barrier, n_dev + n_grp - 2)

    up_g, down_g = lax.rem(g + 1, n_grp), lax.rem(g + n_grp - 1, n_grp)
    up_d, down_d = lax.rem(d + 1, n_dev), lax.rem(d + n_dev - 1, n_dev)
    partners = ((down_g, d), (up_g, d), (g, down_d), (g, up_d))

    def exchange(k, cover=None):
        for half in range(2):
            hi, lo = f_hi[8 * half : 8 * half + 8, :], f_lo[8 * half : 8 * half + 8, :]
            got = pick(lambda c, r: w_t[c * ROWS + r : c * ROWS + r + 1, :], ROWS, hi, lo, 3)
            for c in range(3):
                send[k, 2 * half, 4 * c : 4 * c + 4, :] = got[c][0:4]
                send[k, 2 * half + 1, 4 * c : 4 * c + 4, :] = got[c][4:8]
        copies = []
        for f in range(4):
            copy = pltpu.make_async_remote_copy(
                src_ref=send.at[k, f],
                dst_ref=recv.at[k, f ^ 1],
                send_sem=send_sem.at[k, f],
                recv_sem=recv_sem.at[k, f ^ 1],
                device_id=partners[f],
                device_id_type=MESH,
            )
            copy.start()
            copies.append(copy)
        if cover is not None:
            cover()
        for f in range(4):
            copies[f].wait()
        for q in range(4):
            hi, lo = v_hi[8 * q : 8 * q + 8, :], v_lo[8 * q : 8 * q + 8, :]
            got = pick(
                lambda c, r: recv[k, r // 4, 4 * c + r % 4 : 4 * c + r % 4 + 1, :], 16, hi, lo, 3
            )
            for c in range(3):
                at = slice(c * ROWS + 8 * q, c * ROWS + 8 * q + 8)
                w_t[at, :] = w_t[at, :] + got[c]

    def operate(k):
        def body(v, carry):
            row = pl.multiple_of(8 * (v // 4), 8)
            lane = pl.multiple_of(128 * (v % 4), 128)
            hi, lo = hi_i[pl.ds(row, 8), pl.ds(lane, 128)], lo_i[pl.ds(row, 8), pl.ds(lane, 128)]
            got = pick(lambda c, r: z_t[c * ROWS + r : c * ROWS + r + 1, :], ROWS, hi, lo, 3)
            for c in range(3):
                gath[pl.ds(row + 32 * c, 8), pl.ds(lane, 128)] = got[c]
            return carry

        lax.fori_loop(0, 16, body, 0)
        gh, gl = split(gath[...])
        both = dot(m_hl[...], gh, NN)
        product = both[0:96] + both[96:192] + dot(m_hl[0:96, :], gl, NN)
        put_product(product * coef)
        w_t[...] = mass_t[...] * z_t[...] + scatter()
        exchange(k)

    def make_interpolation():
        home = 6 * (n_dev * g + d)

        def body(q, carry):
            at = pl.ds(pl.multiple_of(512 * q, 512), 512)
            number = lax.broadcasted_iota(I32, (WIN, 512), 0)
            total = jnp.zeros((WIN, 512), F32)
            for j in range(4):
                rel = cn_ref[j : j + 1, at] - home
                rel = jnp.where(rel < 0, rel + CN, rel)
                hit = jnp.broadcast_to(rel, (WIN, 512)) == number
                total = total + jnp.where(hit, jnp.broadcast_to(cw_ref[j : j + 1, at], (WIN, 512)), 0.0)
            high, low = split(total)
            pwh[:, at] = high
            pwl[:, at] = low
            return carry

        lax.fori_loop(0, 8, body, 0)

    exchange(0, make_interpolation)
    dinv_t[...] = DAMPING / w_t[...]
    z_t[...] = rhs_t[...] * dinv_t[...]
    operate(1)
    z_t[...] = z_t[...] + (rhs_t[...] - w_t[...]) * dinv_t[...]
    operate(2)

    w_t[...] = rhs_t[...] - w_t[...]
    flat[...] = jnp.zeros((8, 4096), F32)
    for c in range(3):
        for r in range(ROWS):
            flat[c : c + 1, 128 * r : 128 * r + 128] = w_t[c * ROWS + r : c * ROWS + r + 1, :]
    rh, rl = split(flat[0:8, :])
    left = jnp.concatenate([rh, rl], axis=0)
    first = dot(left, pwh[...], NT)
    window = first[0:8] + first[8:16] + dot(rh, pwl[...], NT)
    offset = 96 * g - 128 * block0 + 6 * d
    shift = lax.broadcasted_iota(I32, (WIN, 256), 1) == lax.broadcasted_iota(I32, (WIN, 256), 0) + offset
    shift = jnp.where(shift, 1.0, 0.0)
    s1_send[...] = dot_exact(window, shift, NN)[0:4]

    def to_all(src, dst, send_sems, recv_sems, along_dev):
        copies = []
        for k in range(1, n_dev if along_dev else n_grp):
            if along_dev:
                target, slot = (g, lax.rem(d + k, n_dev)), k
            else:
                target, slot = (lax.rem(g + k, n_grp), d), k
            copy = pltpu.make_async_remote_copy(
                src_ref=src,
                dst_ref=dst.at[slot],
                send_sem=send_sems.at[k],
                recv_sem=recv_sems.at[k],
                device_id=target,
                device_id_type=MESH,
            )
            copy.start()
            copies.append(copy)
        for copy in copies:
            copy.wait()

    to_all(s1_send, s1_recv, s1_ss, s1_rs, True)
    span = s1_send[...]
    for k in range(1, n_dev):
        span = span + s1_recv[k]
    for copy in l_copies:
        copy.wait()
    acc = jnp.zeros((RB, 128), F32)
    for c in range(3):
        for b in range(2):
            acc = acc + lblk[2 * c + b] * span[c : c + 1, 128 * b : 128 * b + 128]
    s2_send[...] = dot_exact(jnp.ones((8, 128), F32), acc, NT)[0:1]
    to_all(s2_send, s2_recv, s2_ss, s2_rs, False)
    halfway = s2_send[...]
    for k in range(1, n_grp):
        halfway = halfway + s2_recv[k]
    halfway = jnp.broadcast_to(halfway, (8, RB))
    for c in range(3):
        for b in range(2):
            term = dot_exact(halfway, lblk[2 * c + b], NN)
            s3_send[c : c + 1, 128 * b : 128 * b + 128] = term[0:1]
    s3_send[3:4, :] = jnp.zeros((1, 256), F32)
    to_all(s3_send, s3_recv, s3_ss, s3_rs, True)
    span = s3_send[...]
    for k in range(1, n_dev):
        span = span + s3_recv[k]
    correction = dot_exact(jnp.concatenate([span, span], axis=0), shift, NT)
    ch, cl = split(correction)
    left = jnp.concatenate([ch, cl], axis=0)
    first = dot(left, pwh[...], NN)
    flat[0:8, :] = first[0:8] + first[8:16] + dot(ch, pwl[...], NN)
    for c in range(3):
        for r in range(ROWS):
            at = slice(c * ROWS + r, c * ROWS + r + 1)
            z_t[at, :] = z_t[at, :] + flat[c : c + 1, 128 * r : 128 * r + 128]

    operate(3)
    z_t[...] = z_t[...] + (rhs_t[...] - w_t[...]) * dinv_t[...]
    operate(4)
    z_t[...] = z_t[...] + (rhs_t[...] - w_t[...]) * dinv_t[...]
    for c in range(3):
        for r in range(ROWS):
            out_ref[c : c + 1, 128 * r : 128 * r + 128] = z_t[c * ROWS + r : c * ROWS + r + 1, :]


def solution(mesh):
    n_grp, n_dev = mesh.shape["grp"], mesh.shape["dev"]

    def local(rhs, nodes, coef, mass, faces, coarse, weights, matrix, chol):
        vmem = pl.BlockSpec(memory_space=pltpu.VMEM)
        dma = pltpu.SemaphoreType.DMA

        def body(*refs):
            kernel(n_grp, n_dev, *refs)

        out = pl.pallas_call(
            body,
            name="two_level",
            out_shape=jax.ShapeDtypeStruct((3, 4096), F32),
            in_specs=[vmem] * 8 + [pl.BlockSpec(memory_space=pl.ANY)],
            out_specs=vmem,
            scratch_shapes=[
                pltpu.VMEM((96, 128), F32),
                pltpu.VMEM((96, 128), F32),
                pltpu.VMEM((96, 128), F32),
                pltpu.VMEM((96, 128), F32),
                pltpu.VMEM((96, 128), F32),
                pltpu.VMEM((32, ELEM), I32),
                pltpu.VMEM((32, ELEM), I32),
                pltpu.VMEM((96, ELEM), F32),
                pltpu.VMEM((96, ELEM), F32),
                pltpu.VMEM((96, ELEM), F32),
                pltpu.VMEM((192, 96), BF16),
                pltpu.VMEM((NODES_PER, 128, ELEM), BF16),
                pltpu.VMEM((NODES_PER, ROWS, ELEM), BF16),
                pltpu.VMEM((16, 128), I32),
                pltpu.VMEM((16, 128), I32),
                pltpu.VMEM((32, 128), I32),
                pltpu.VMEM((32, 128), I32),
                pltpu.VMEM((WIN, 4096), BF16),
                pltpu.VMEM((WIN, 4096), BF16),
                pltpu.VMEM((8, 4096), F32),
                pltpu.VMEM((5, 4, 16, 128), F32),
                pltpu.VMEM((5, 4, 16, 128), F32),
                pltpu.VMEM((4, 256), F32),
                pltpu.VMEM((n_dev, 4, 256), F32),
                pltpu.VMEM((1, RB), F32),
                pltpu.VMEM((n_grp, 1, RB), F32),
                pltpu.VMEM((4, 256), F32),
                pltpu.VMEM((n_dev, 4, 256), F32),
                pltpu.VMEM((6, RB, 128), F32),
                dma((5, 4)), dma((5, 4)),
                dma((n_dev,)), dma((n_dev,)),
                dma((n_grp,)), dma((n_grp,)),
                dma((n_dev,)), dma((n_dev,)),
                dma((6,)),
            ],
            compiler_params=pltpu.CompilerParams(
                collective_id=0, has_side_effects=True, vmem_limit_bytes=48 << 20
            ),
        )(
            rhs[0, 0], nodes[0, 0], coef[0], mass[0, 0], faces[0, 0], coarse[0, 0],
            weights[0, 0], matrix, chol,
        )
        return out[None, None]

    return jax.shard_map(
        local,
        mesh=mesh,
        in_specs=(
            P("grp", "dev", None, None),
            P("grp", "dev", None, None),
            P("grp", "dev", None),
            P("grp", "dev", None, None),
            P("grp", "dev", None, None),
            P("grp", "dev", None, None),
            P("grp", "dev", None, None),
            P(),
            P("dev", None),
        ),
        out_specs=P("grp", "dev", None, None),
        check_vma=False,
    )
```

```python
import jax
import jax.numpy as jnp
from jax import lax
from jax.experimental import pallas as pl
from jax.experimental.pallas import tpu as pltpu
from jax.sharding import PartitionSpec as P

DAMPING = 0.6
MESH = pl.DeviceIdType.MESH
BF16 = jnp.bfloat16
F32 = jnp.float32
I32 = jnp.int32
NT = (((1,), (1,)), ((), ()))
NN = (((1,), (0,)), ((), ()))

ROWS = 32
NODES_PER = 27
ELEM = 512
CN = 1536
WIN = 64
RB = 288


def dot(a, b, dims):
    return lax.dot_general(a, b, dims, preferred_element_type=F32)


def dot_exact(a, b, dims):
    return lax.dot_general(
        a, b, dims, precision=lax.Precision.HIGHEST, preferred_element_type=F32
    )


def split(x):
    high = x.astype(BF16)
    low = (x - high.astype(F32)).astype(BF16)
    return high, low


def lane_gather(row, lanes):
    return jnp.take_along_axis(row, lanes, axis=1, mode="promise_in_bounds")


def pick(load_row, rows, hi, lo, fields):
    got = [jnp.zeros(hi.shape, F32) for _ in range(fields)]
    for r in range(rows):
        here = hi == r
        for c in range(fields):
            row = jnp.broadcast_to(load_row(c, r), hi.shape)
            got[c] = jnp.where(here, lane_gather(row, lo), got[c])
    return got


def kernel(
    n_grp, n_dev,
    rhs_hbm, nodes_hbm, coef_hbm, mass_hbm, face_hbm, cn_hbm, cw_hbm, em_hbm, chol_ref,
    out_ref,
    z_t, w_t, rhs_t, mass_t, dinv_t, hi_i, lo_i, gath, p_hi, p_lo, m_hl, bt, oh,
    f_hi, f_lo, v_hi, v_lo, pwh, pwl, flat,
    nodes_ref, coef_ref, face_ref, cn_ref, cw_ref, em_ref,
    send, recv, s1_send, s1_recv, s2_send, s2_recv, s3_send, s3_recv, lblk,
    send_sem, recv_sem, s1_ss, s1_rs, s2_ss, s2_rs, s3_ss, s3_rs, l_sem, in_sem,
):
    g = lax.axis_index("grp")
    d = lax.axis_index("dev")

    pairs = (
        (nodes_hbm, nodes_ref), (face_hbm, face_ref), (em_hbm, em_ref), (coef_hbm, coef_ref),
        (mass_hbm, mass_t), (rhs_hbm, rhs_t), (cn_hbm, cn_ref), (cw_hbm, cw_ref),
    )
    loads = [pltpu.make_async_copy(a, b, in_sem.at[j]) for j, (a, b) in enumerate(pairs)]
    for load in loads:
        load.start()

    block0 = (3 * g) // 4
    block1 = lax.rem(block0 + 1, CN // 128)
    l_copies = []
    for c in range(3):
        for b, block in enumerate((block0, block1)):
            at = pl.multiple_of(CN * c + 128 * block, 128)
            copy = pltpu.make_async_copy(
                chol_ref.at[:, pl.ds(at, 128)], lblk.at[2 * c + b], l_sem.at[2 * c + b]
            )
            copy.start()
            l_copies.append(copy)

    barrier = pltpu.get_barrier_semaphore()
    for k in range(1, n_dev):
        pl.semaphore_signal(
            barrier, inc=1, device_id=(g, lax.rem(d + k, n_dev)), device_id_type=MESH
        )
    for k in range(1, n_grp):
        pl.semaphore_signal(
            barrier, inc=1, device_id=(lax.rem(g + k, n_grp), d), device_id_type=MESH
        )

    for load in loads:
        load.wait()
    for f in range(4):
        for r in range(4):
            face = face_ref[f : f + 1, 128 * r : 128 * r + 128]
            f_hi[4 * f + r : 4 * f + r + 1, :] = face >> 7
            f_lo[4 * f + r : 4 * f + r + 1, :] = face & 127

    hi_i[...] = jnp.zeros((32, ELEM), I32)
    lo_i[...] = jnp.zeros((32, ELEM), I32)
    for i in range(NODES_PER):
        for k in range(4):
            index = nodes_ref[i, k : k + 1, :]
            hi_i[i : i + 1, 128 * k : 128 * k + 128] = index >> 7
            lo_i[i : i + 1, 128 * k : 128 * k + 128] = index & 127

    def one_hot(index_row, count):
        at = jnp.broadcast_to(index_row, (count, index_row.shape[1]))
        number = lax.broadcasted_iota(I32, at.shape, 0)
        return jnp.where(at == number, 1.0, 0.0).astype(BF16)

    def make_one_hot(i, carry):
        oh[i] = one_hot(hi_i[pl.ds(i, 1), :], ROWS)
        bt[:, pl.ds(pl.multiple_of(ELEM * i, ELEM), ELEM)] = one_hot(lo_i[pl.ds(i, 1), :], 128)
        return carry

    lax.fori_loop(0, NODES_PER, make_one_hot, 0)

    row_of = lax.broadcasted_iota(I32, (96, 81), 0)
    col_of = lax.broadcasted_iota(I32, (96, 81), 1)
    place = (col_of == 27 * (row_of // 32) + row_of % 32) & (row_of % 32 < 27)
    place = jnp.where(place, 1.0, 0.0)
    matrix = dot_exact(dot_exact(place, em_ref[...], NN), place, NT)
    mh, ml = split(matrix)
    m_hl[0:96, :] = mh
    m_hl[96:192, :] = ml
    eye = lax.broadcasted_iota(I32, (96, 96), 0) == lax.broadcasted_iota(I32, (96, 96), 1)
    main_diag = jnp.sum(jnp.where(eye, matrix, 0.0), axis=1, keepdims=True)
    coef = coef_ref[...]

    def put_product(product):
        high = product.astype(BF16).astype(F32)
        p_hi[...] = high
        p_lo[...] = product - high

    def scatter():
        columns = []
        for i in range(NODES_PER):
            hot = oh[i]
            blocks = []
            for part in (p_hi, p_lo):
                for c in range(3):
                    row = part[c * 32 + i : c * 32 + i + 1, :]
                    value = jnp.broadcast_to(row, (ROWS, ELEM)).astype(BF16)
                    blocks.append(value * hot)
            columns.append(jnp.concatenate(blocks, axis=0))
        acc = dot(jnp.concatenate(columns, axis=1), bt[...], NT)
        return acc[0:96] + acc[96:192]

    acc = jnp.zeros((64, 128), F32)
    for f in range(4):
        face = face_ref[f : f + 1, :]
        hot = one_hot(face >> 7, ROWS)
        slot = lax.broadcasted_iota(I32, (ROWS, ELEM), 1) + (512 * f + 1)
        a = jnp.concatenate(
            [(slot >> 6).astype(F32).astype(BF16) * hot, (slot & 63).astype(F32).astype(BF16) * hot],
            axis=0,
        )
        acc = acc + dot(a, one_hot(face & 127, 128), NT)
    inverse = (64.0 * acc[0:32] + acc[32:64]).astype(I32) - 1
    v_hi[...] = inverse >> 7
    v_lo[...] = inverse & 127

    put_product(main_diag * coef)
    w_t[...] = mass_t[...] + scatter()

    pl.semaphore_wait(barrier, n_dev + n_grp - 2)

    up_g, down_g = lax.rem(g + 1, n_grp), lax.rem(g + n_grp - 1, n_grp)
    up_d, down_d = lax.rem(d + 1, n_dev), lax.rem(d + n_dev - 1, n_dev)
    partners = ((down_g, d), (up_g, d), (g, down_d), (g, up_d))

    def exchange(k, cover=None):
        for half in range(2):
            hi, lo = f_hi[8 * half : 8 * half + 8, :], f_lo[8 * half : 8 * half + 8, :]
            got = pick(lambda c, r: w_t[c * ROWS + r : c * ROWS + r + 1, :], ROWS, hi, lo, 3)
            for c in range(3):
                send[k, 2 * half, c] = got[c][0:4]
                send[k, 2 * half + 1, c] = got[c][4:8]
        copies = []
        for f in range(4):
            copy = pltpu.make_async_remote_copy(
                src_ref=send.at[k, f],
                dst_ref=recv.at[k, f ^ 1],
                send_sem=send_sem.at[k, f],
                recv_sem=recv_sem.at[k, f ^ 1],
                device_id=partners[f],
                device_id_type=MESH,
            )
            copy.start()
            copies.append(copy)
        if cover is not None:
            cover()
        for f in range(4):
            copies[f].wait()
        for q in range(4):
            hi, lo = v_hi[8 * q : 8 * q + 8, :], v_lo[8 * q : 8 * q + 8, :]
            got = pick(
                lambda c, r: recv[k, r // 4, c, r % 4 : r % 4 + 1, :], 16, hi, lo, 3
            )
            for c in range(3):
                at = slice(c * ROWS + 8 * q, c * ROWS + 8 * q + 8)
                w_t[at, :] = w_t[at, :] + got[c]

    def operate(k):
        def body(v, carry):
            row = pl.multiple_of(8 * (v // 4), 8)
            lane = pl.multiple_of(128 * (v % 4), 128)
            hi, lo = hi_i[pl.ds(row, 8), pl.ds(lane, 128)], lo_i[pl.ds(row, 8), pl.ds(lane, 128)]
            got = pick(lambda c, r: z_t[c * ROWS + r : c * ROWS + r + 1, :], ROWS, hi, lo, 3)
            for c in range(3):
                gath[pl.ds(row + 32 * c, 8), pl.ds(lane, 128)] = got[c]
            return carry

        lax.fori_loop(0, 16, body, 0, unroll=4)
        gh, gl = split(gath[...])
        both = dot(m_hl[...], gh, NN)
        product = both[0:96] + both[96:192] + dot(m_hl[0:96, :], gl, NN)
        put_product(product * coef)
        w_t[...] = mass_t[...] * z_t[...] + scatter()
        exchange(k)

    def make_interpolation():
        home = 6 * (n_dev * g + d)

        def body(q, carry):
            at = pl.ds(pl.multiple_of(512 * q, 512), 512)
            number = lax.broadcasted_iota(I32, (WIN, 512), 0)
            total = jnp.zeros((WIN, 512), F32)
            for j in range(4):
                rel = cn_ref[j : j + 1, at] - home
                rel = jnp.where(rel < 0, rel + CN, rel)
                hit = jnp.broadcast_to(rel, (WIN, 512)) == number
                total = total + jnp.where(hit, jnp.broadcast_to(cw_ref[j : j + 1, at], (WIN, 512)), 0.0)
            high, low = split(total)
            pwh[:, at] = high
            pwl[:, at] = low
            return carry

        lax.fori_loop(0, 8, body, 0)

    exchange(0, make_interpolation)
    dinv_t[...] = DAMPING / w_t[...]
    z_t[...] = rhs_t[...] * dinv_t[...]
    operate(1)
    z_t[...] = z_t[...] + (rhs_t[...] - w_t[...]) * dinv_t[...]
    operate(2)

    w_t[...] = rhs_t[...] - w_t[...]
    flat[...] = jnp.zeros((8, 4096), F32)
    for c in range(3):
        for r in range(ROWS):
            flat[c : c + 1, 128 * r : 128 * r + 128] = w_t[c * ROWS + r : c * ROWS + r + 1, :]
    rh, rl = split(flat[0:8, :])
    left = jnp.concatenate([rh, rl], axis=0)
    first = dot(left, pwh[...], NT)
    window = first[0:8] + first[8:16] + dot(rh, pwl[...], NT)
    for c in range(3):
        s1_send[:, WIN * c : WIN * c + WIN] = window[c : c + 1]
    s1_send[:, 3 * WIN :] = jnp.zeros((1, 256 - 3 * WIN), F32)
    s1_recv[d] = s1_send[...]
    lane = lax.broadcasted_iota(I32, (n_dev, 128), 1)
    first_at = 6 * lax.broadcasted_iota(I32, (n_dev, 128), 0) + (96 * g - 128 * block0)

    def to_all(src, dst, send_sems, recv_sems, along_dev):
        me, count = (d, n_dev) if along_dev else (g, n_grp)
        copies = []
        for k in range(1, count):
            peer = lax.rem(me + k, count)
            copy = pltpu.make_async_remote_copy(
                src_ref=src(peer),
                dst_ref=dst.at[me],
                send_sem=send_sems.at[k],
                recv_sem=recv_sems.at[k],
                device_id=(g, peer) if along_dev else (peer, d),
                device_id_type=MESH,
            )
            copy.start()
            copies.append(copy)
        for copy in copies:
            copy.wait()

    to_all(lambda peer: s1_send, s1_recv, s1_ss, s1_rs, True)
    windows = s1_recv[:, 0, :]
    span = []
    for c in range(3):
        row = []
        for b in range(2):
            at = lane + 128 * b - first_at
            inside = (at >= 0) & (at < WIN)
            at = jnp.where(inside, at, 0) + WIN * (c % 2)
            values = lane_gather(windows[:, 128 * (c // 2) : 128 * (c // 2) + 128], at)
            row.append(jnp.sum(jnp.where(inside, values, 0.0), axis=0, keepdims=True))
        span.append(row)
    for copy in l_copies:
        copy.wait()
    acc = jnp.zeros((RB, 128), F32)
    for c in range(3):
        for b in range(2):
            acc = acc + lblk[2 * c + b] * span[c][b]
    s2_send[...] = dot_exact(jnp.ones((8, 128), F32), acc, NT)[0:1]
    s2_recv[g] = s2_send[...]
    to_all(lambda peer: s2_send, s2_recv, s2_ss, s2_rs, False)
    halfway = jnp.sum(s2_recv[:, 0, :], axis=0, keepdims=True)
    halfway = jnp.broadcast_to(halfway, (8, RB))
    parts = []
    for c in range(3):
        at = jnp.where(lane < WIN, lane, lane - WIN) + first_at
        values = []
        for b in range(2):
            row = dot_exact(halfway, lblk[2 * c + b], NN)[0:1]
            values.append(
                lane_gather(jnp.broadcast_to(row, (n_dev, 128)), jnp.clip(at - 128 * b, 0, 127))
            )
        parts.append(jnp.where(at < 128, values[0], values[1]))
    s3_send[:, 0, 0:128] = jnp.where(lane < WIN, parts[0], parts[1])
    s3_send[:, 0, 128:256] = parts[2]
    s3_recv[d] = s3_send[d]
    to_all(lambda peer: s3_send.at[peer], s3_recv, s3_ss, s3_rs, True)
    total = jnp.sum(s3_recv[:, 0, :], axis=0, keepdims=True)
    correction = jnp.concatenate(
        [total[:, WIN * c : WIN * c + WIN] for c in range(3)] + [jnp.zeros((5, WIN), F32)], axis=0
    )
    ch, cl = split(correction)
    left = jnp.concatenate([ch, cl], axis=0)
    first = dot(left, pwh[...], NN)
    flat[0:8, :] = first[0:8] + first[8:16] + dot(ch, pwl[...], NN)
    for c in range(3):
        for r in range(ROWS):
            at = slice(c * ROWS + r, c * ROWS + r + 1)
            z_t[at, :] = z_t[at, :] + flat[c : c + 1, 128 * r : 128 * r + 128]

    operate(3)
    z_t[...] = z_t[...] + (rhs_t[...] - w_t[...]) * dinv_t[...]
    operate(4)
    out_ref[...] = z_t[...] + (rhs_t[...] - w_t[...]) * dinv_t[...]


def solution(mesh):
    n_grp, n_dev = mesh.shape["grp"], mesh.shape["dev"]

    def local(rhs, nodes, coef, mass, faces, coarse, weights, matrix, chol):
        dma = pltpu.SemaphoreType.DMA

        def body(*refs):
            kernel(n_grp, n_dev, *refs)

        out = pl.pallas_call(
            body,
            name="two_level",
            out_shape=jax.ShapeDtypeStruct((96, 128), F32),
            in_specs=[pl.BlockSpec(memory_space=pltpu.HBM)] * 9,
            out_specs=pl.BlockSpec(memory_space=pltpu.VMEM),
            scratch_shapes=[
                pltpu.VMEM((96, 128), F32),
                pltpu.VMEM((96, 128), F32),
                pltpu.VMEM((96, 128), F32),
                pltpu.VMEM((96, 128), F32),
                pltpu.VMEM((96, 128), F32),
                pltpu.VMEM((32, ELEM), I32),
                pltpu.VMEM((32, ELEM), I32),
                pltpu.VMEM((96, ELEM), F32),
                pltpu.VMEM((96, ELEM), F32),
                pltpu.VMEM((96, ELEM), F32),
                pltpu.VMEM((192, 96), BF16),
                pltpu.VMEM((128, NODES_PER * ELEM), BF16),
                pltpu.VMEM((NODES_PER, ROWS, ELEM), BF16),
                pltpu.VMEM((16, 128), I32),
                pltpu.VMEM((16, 128), I32),
                pltpu.VMEM((32, 128), I32),
                pltpu.VMEM((32, 128), I32),
                pltpu.VMEM((WIN, 4096), BF16),
                pltpu.VMEM((WIN, 4096), BF16),
                pltpu.VMEM((8, 4096), F32),
                pltpu.VMEM((27, 4, 128), I32),
                pltpu.VMEM((1, ELEM), F32),
                pltpu.VMEM((4, 512), I32),
                pltpu.VMEM((4, 4096), I32),
                pltpu.VMEM((4, 4096), F32),
                pltpu.VMEM((81, 81), F32),
                pltpu.VMEM((5, 4, 3, 4, 128), F32),
                pltpu.VMEM((5, 4, 3, 4, 128), F32),
                pltpu.VMEM((1, 256), F32),
                pltpu.VMEM((n_dev, 1, 256), F32),
                pltpu.VMEM((1, RB), F32),
                pltpu.VMEM((n_grp, 1, RB), F32),
                pltpu.VMEM((n_dev, 1, 256), F32),
                pltpu.VMEM((n_dev, 1, 256), F32),
                pltpu.VMEM((6, RB, 128), F32),
                dma((5, 4)), dma((5, 4)),
                dma((n_dev,)), dma((n_dev,)),
                dma((n_grp,)), dma((n_grp,)),
                dma((n_dev,)), dma((n_dev,)),
                dma((6,)),
                dma((8,)),
            ],
            compiler_params=pltpu.CompilerParams(
                collective_id=0, has_side_effects=True, vmem_limit_bytes=67_000_000
            ),
        )(
            rhs.reshape(96, 128), nodes.reshape(27, 4, 128), coef[0], mass.reshape(96, 128),
            faces[0, 0], coarse[0, 0], weights[0, 0], matrix, chol,
        )
        return out.reshape(1, 1, 3, 4096)

    return jax.shard_map(
        local,
        mesh=mesh,
        in_specs=(
            P("grp", "dev", None, None),
            P("grp", "dev", None, None),
            P("grp", "dev", None),
            P("grp", "dev", None, None),
            P("grp", "dev", None, None),
            P("grp", "dev", None, None),
            P("grp", "dev", None, None),
            P(),
            P("dev", None),
        ),
        out_specs=P("grp", "dev", None, None),
        check_vma=False,
    )
```

```python
import jax
import jax.numpy as jnp
from jax import lax
from jax.experimental import pallas as pl
from jax.experimental.pallas import tpu as pltpu
from jax.sharding import PartitionSpec as P

DAMPING = 0.6
MESH = pl.DeviceIdType.MESH
BF16 = jnp.bfloat16
F32 = jnp.float32
I32 = jnp.int32
NT = (((1,), (1,)), ((), ()))
NN = (((1,), (0,)), ((), ()))

ROWS = 32
FROWS = 16
NODES_PER = 27
ELEM = 512
CN = 1536
WIN = 64
RB = 288


def dot(a, b, dims):
    return lax.dot_general(a, b, dims, preferred_element_type=F32)


def dot_exact(a, b, dims):
    return lax.dot_general(
        a, b, dims, precision=lax.Precision.HIGHEST, preferred_element_type=F32
    )


def split(x):
    high = x.astype(BF16)
    low = (x - high.astype(F32)).astype(BF16)
    return high, low


def lane_gather(row, lanes):
    return jnp.take_along_axis(row, lanes, axis=1, mode="promise_in_bounds")


def pick(load_row, rows, hi, lo, start):
    got = list(start)
    fields = len(got)
    for r in range(rows):
        here = hi == r
        for c in range(fields):
            row = jnp.broadcast_to(load_row(c, r), hi.shape)
            got[c] = jnp.where(here, lane_gather(row, lo), got[c])
    return got


def kernel(
    n_grp, n_dev,
    rhs_hbm, nodes_hbm, coef_hbm, mass_hbm, face_hbm, cn_hbm, cw_hbm, em_hbm, chol_ref,
    out_ref,
    zf, zi, wf, wi, rf, ri, mf, mi, df, di,
    hi_i, lo_i, gath, p_hi, p_lo, m_hl, bn, oh,
    f_hi, f_lo, v_hi, v_lo, inv_t, pwh, pwl, flat,
    nodes_ref, coef_ref, face_ref, cn_ref, cw_ref, em_ref,
    send, recv, s1_send, s1_recv, s2_send, s2_recv, s3_send, s3_recv, lblk,
    send_sem, recv_sem, s1_ss, s1_rs, s2_ss, s2_rs, s3_ss, s3_rs, l_sem, in_sem,
):
    g = lax.axis_index("grp")
    d = lax.axis_index("dev")

    pairs = (
        (nodes_hbm, nodes_ref), (face_hbm, face_ref), (em_hbm, em_ref), (coef_hbm, coef_ref),
        (mass_hbm, mi), (rhs_hbm, ri), (cn_hbm, cn_ref), (cw_hbm, cw_ref),
    )
    loads = [pltpu.make_async_copy(a, b, in_sem.at[j]) for j, (a, b) in enumerate(pairs)]
    for load in loads:
        load.start()

    block0 = (3 * g) // 4
    block1 = lax.rem(block0 + 1, CN // 128)
    l_copies = []
    for c in range(3):
        for b, block in enumerate((block0, block1)):
            at = pl.multiple_of(CN * c + 128 * block, 128)
            copy = pltpu.make_async_copy(
                chol_ref.at[:, pl.ds(at, 128)], lblk.at[2 * c + b], l_sem.at[2 * c + b]
            )
            copy.start()
            l_copies.append(copy)

    barrier = pltpu.get_barrier_semaphore()
    for k in range(1, n_dev):
        pl.semaphore_signal(
            barrier, inc=1, device_id=(g, lax.rem(d + k, n_dev)), device_id_type=MESH
        )
    for k in range(1, n_grp):
        pl.semaphore_signal(
            barrier, inc=1, device_id=(lax.rem(g + k, n_grp), d), device_id_type=MESH
        )

    for load in loads:
        load.wait()
    for f in range(4):
        for r in range(4):
            face = face_ref[f : f + 1, 128 * r : 128 * r + 128]
            f_hi[4 * f + r : 4 * f + r + 1, :] = face >> 7
            f_lo[4 * f + r : 4 * f + r + 1, :] = face & 127

    def one_hot(index_row, count):
        at = jnp.broadcast_to(index_row, (count, index_row.shape[1]))
        number = lax.broadcasted_iota(I32, at.shape, 0)
        return jnp.where(at == number, 1.0, 0.0).astype(BF16)

    acc = jnp.zeros((64, 128), F32)
    for f in range(4):
        face = face_ref[f : f + 1, :]
        hot = one_hot(face >> 7, ROWS)
        slot = lax.broadcasted_iota(I32, (ROWS, ELEM), 1) + (512 * f + 1)
        a = jnp.concatenate(
            [(slot >> 6).astype(F32).astype(BF16) * hot, (slot & 63).astype(F32).astype(BF16) * hot],
            axis=0,
        )
        acc = acc + dot(a, one_hot(face & 127, 128), NT)
    inverse = (64.0 * acc[0:32] + acc[32:64]).astype(I32) - 1
    inv_t[...] = inverse
    v_hi[...] = inverse >> 7
    v_lo[...] = inverse & 127

    hi_i[...] = jnp.zeros((32, ELEM), I32)
    lo_i[...] = jnp.zeros((32, ELEM), I32)
    for i in range(NODES_PER):
        for k in range(4):
            index = nodes_ref[i, k : k + 1, :]
            hi_i[i : i + 1, 128 * k : 128 * k + 128] = index >> 7
            lo_i[i : i + 1, 128 * k : 128 * k + 128] = index & 127

    def renumber(v, carry):
        row = pl.multiple_of(8 * (v // 4), 8)
        lane = pl.multiple_of(128 * (v % 4), 128)
        at = (pl.ds(row, 8), pl.ds(lane, 128))
        hi, lo = hi_i[at], lo_i[at]
        slot = pick(lambda c, r: inv_t[r : r + 1, :], ROWS, hi, lo, [jnp.full((8, 128), -1, I32)])[0]
        hi_i[at] = jnp.where(slot >= 0, slot >> 7, hi + FROWS)
        lo_i[at] = jnp.where(slot >= 0, slot & 127, lo)
        return carry

    lax.fori_loop(0, 16, renumber, 0, unroll=4)

    def make_one_hot(i, carry):
        oh[i] = one_hot(hi_i[pl.ds(i, 1), :], FROWS + ROWS)
        return carry

    lax.fori_loop(0, NODES_PER, make_one_hot, 0)
    turned = lo_i[...].astype(F32).T
    number = lax.broadcasted_iota(I32, (ELEM, 128), 1).astype(F32)
    for i in range(NODES_PER):
        same = jnp.broadcast_to(turned[:, i : i + 1], (ELEM, 128)) == number
        bn[ELEM * i : ELEM * i + ELEM, :] = jnp.where(same, 1.0, 0.0).astype(BF16)

    for half in range(2):
        hi, lo = f_hi[8 * half : 8 * half + 8, :], f_lo[8 * half : 8 * half + 8, :]
        for source, target, idle in ((mi, mf, 1.0), (ri, rf, 0.0)):
            got = pick(
                lambda c, r: source[c * ROWS + r : c * ROWS + r + 1, :], ROWS, hi, lo,
                [jnp.full((8, 128), idle, F32)] * 3,
            )
            for c in range(3):
                target[c * FROWS + 8 * half : c * FROWS + 8 * half + 8, :] = got[c]

    row_of = lax.broadcasted_iota(I32, (96, 81), 0)
    col_of = lax.broadcasted_iota(I32, (96, 81), 1)
    place = (col_of == 27 * (row_of // 32) + row_of % 32) & (row_of % 32 < 27)
    place = jnp.where(place, 1.0, 0.0)
    matrix = dot_exact(dot_exact(place, em_ref[...], NN), place, NT)
    mh, ml = split(matrix)
    m_hl[0:96, :] = mh
    m_hl[96:192, :] = ml
    eye = lax.broadcasted_iota(I32, (96, 96), 0) == lax.broadcasted_iota(I32, (96, 96), 1)
    main_diag = jnp.sum(jnp.where(eye, matrix, 0.0), axis=1, keepdims=True)
    coef = coef_ref[...]

    def put_product(product):
        high = product.astype(BF16).astype(F32)
        p_hi[...] = high
        p_lo[...] = product - high

    def scatter(first, rows):
        columns = []
        for i in range(NODES_PER):
            hot = oh[i, first : first + rows]
            blocks = []
            for part in (p_hi, p_lo):
                for c in range(3):
                    row = part[c * 32 + i : c * 32 + i + 1, :]
                    value = jnp.broadcast_to(row, (rows, ELEM)).astype(BF16)
                    blocks.append(value * hot)
            columns.append(jnp.concatenate(blocks, axis=0))
        acc = dot(jnp.concatenate(columns, axis=1), bn[...], NN)
        return acc[0 : 3 * rows] + acc[3 * rows : 6 * rows]

    put_product(main_diag * coef)
    wf[...] = mf[...] + scatter(0, FROWS)

    pl.semaphore_wait(barrier, n_dev + n_grp - 2)

    up_g, down_g = lax.rem(g + 1, n_grp), lax.rem(g + n_grp - 1, n_grp)
    up_d, down_d = lax.rem(d + 1, n_dev), lax.rem(d + n_dev - 1, n_dev)
    partners = ((down_g, d), (up_g, d), (g, down_d), (g, up_d))

    def send_faces(k):
        for f in range(4):
            for c in range(3):
                send[k, f, c] = wf[c * FROWS + 4 * f : c * FROWS + 4 * f + 4, :]
        copies = []
        for f in range(4):
            copy = pltpu.make_async_remote_copy(
                src_ref=send.at[k, f],
                dst_ref=recv.at[k, f ^ 1],
                send_sem=send_sem.at[k, f],
                recv_sem=recv_sem.at[k, f ^ 1],
                device_id=partners[f],
                device_id_type=MESH,
            )
            copy.start()
            copies.append(copy)
        return copies

    def add_faces(k, copies):
        for copy in copies:
            copy.wait()
        for f in range(4):
            for c in range(3):
                at = slice(c * FROWS + 4 * f, c * FROWS + 4 * f + 4)
                wf[at, :] = wf[at, :] + recv[k, f, c]

    def gather(table, first, rows, fresh):
        def body(v, carry):
            row = pl.multiple_of(8 * (v // 4), 8)
            lane = pl.multiple_of(128 * (v % 4), 128)
            hi, lo = hi_i[pl.ds(row, 8), pl.ds(lane, 128)], lo_i[pl.ds(row, 8), pl.ds(lane, 128)]
            if fresh:
                start = [jnp.zeros((8, 128), F32)] * 3
            else:
                start = [gath[pl.ds(row + 32 * c, 8), pl.ds(lane, 128)] for c in range(3)]
            got = pick(
                lambda c, r: table[c * rows + r : c * rows + r + 1, :], rows, hi - first, lo, start
            )
            for c in range(3):
                gath[pl.ds(row + 32 * c, 8), pl.ds(lane, 128)] = got[c]
            return carry

        lax.fori_loop(0, 16, body, 0, unroll=8)

    def gather_interior():
        gather(zi, FROWS, ROWS, True)

    def gather_faces():
        gather(zf, 0, FROWS, False)

    def operate(k, interior):
        gh, gl = split(gath[...])
        both = dot(m_hl[...], gh, NN)
        product = both[0:96] + both[96:192] + dot(m_hl[0:96, :], gl, NN)
        put_product(product * coef)
        wf[...] = mf[...] * zf[...] + scatter(0, FROWS)
        copies = send_faces(k)
        wi[...] = mi[...] * zi[...] + scatter(FROWS, ROWS)
        interior()
        add_faces(k, copies)

    def step_interior():
        zi[...] = zi[...] + (ri[...] - wi[...]) * di[...]
        gather_interior()

    def step_faces():
        zf[...] = zf[...] + (rf[...] - wf[...]) * df[...]
        gather_faces()

    def make_interpolation():
        home = 6 * (n_dev * g + d)

        def body(q, carry):
            at = pl.ds(pl.multiple_of(512 * q, 512), 512)
            number = lax.broadcasted_iota(I32, (WIN, 512), 0)
            total = jnp.zeros((WIN, 512), F32)
            for j in range(4):
                rel = cn_ref[j : j + 1, at] - home
                rel = jnp.where(rel < 0, rel + CN, rel)
                hit = jnp.broadcast_to(rel, (WIN, 512)) == number
                total = total + jnp.where(hit, jnp.broadcast_to(cw_ref[j : j + 1, at], (WIN, 512)), 0.0)
            high, low = split(total)
            pwh[:, at] = high
            pwl[:, at] = low
            return carry

        lax.fori_loop(0, 8, body, 0)

    copies = send_faces(0)
    wi[...] = mi[...] + scatter(FROWS, ROWS)
    di[...] = DAMPING / wi[...]
    zi[...] = ri[...] * di[...]
    gather_interior()
    add_faces(0, copies)
    df[...] = DAMPING / wf[...]
    zf[...] = rf[...] * df[...]
    gather_faces()
    operate(1, step_interior)
    step_faces()
    operate(2, make_interpolation)

    wf[...] = rf[...] - wf[...]
    flat[...] = jnp.zeros((8, 4096), F32)
    for q in range(4):
        hi, lo = v_hi[8 * q : 8 * q + 8, :], v_lo[8 * q : 8 * q + 8, :]
        rows = [slice(c * ROWS + 8 * q, c * ROWS + 8 * q + 8) for c in range(3)]
        got = pick(
            lambda c, r: wf[c * FROWS + r : c * FROWS + r + 1, :], FROWS, hi, lo,
            [ri[at, :] - wi[at, :] for at in rows],
        )
        for c in range(3):
            wi[rows[c], :] = got[c]
    for c in range(3):
        for r in range(ROWS):
            flat[c : c + 1, 128 * r : 128 * r + 128] = wi[c * ROWS + r : c * ROWS + r + 1, :]
    rh, rl = split(flat[0:8, :])
    left = jnp.concatenate([rh, rl], axis=0)
    first = dot(left, pwh[...], NT)
    window = first[0:8] + first[8:16] + dot(rh, pwl[...], NT)
    for c in range(3):
        s1_send[:, WIN * c : WIN * c + WIN] = window[c : c + 1]
    s1_send[:, 3 * WIN :] = jnp.zeros((1, 256 - 3 * WIN), F32)
    s1_recv[d] = s1_send[...]
    lane = lax.broadcasted_iota(I32, (n_dev, 128), 1)
    first_at = 6 * lax.broadcasted_iota(I32, (n_dev, 128), 0) + (96 * g - 128 * block0)

    def to_all(src, dst, send_sems, recv_sems, along_dev):
        me, count = (d, n_dev) if along_dev else (g, n_grp)
        copies = []
        for k in range(1, count):
            peer = lax.rem(me + k, count)
            copy = pltpu.make_async_remote_copy(
                src_ref=src(peer),
                dst_ref=dst.at[me],
                send_sem=send_sems.at[k],
                recv_sem=recv_sems.at[k],
                device_id=(g, peer) if along_dev else (peer, d),
                device_id_type=MESH,
            )
            copy.start()
            copies.append(copy)
        for copy in copies:
            copy.wait()

    to_all(lambda peer: s1_send, s1_recv, s1_ss, s1_rs, True)
    windows = s1_recv[:, 0, :]
    span = []
    for c in range(3):
        row = []
        for b in range(2):
            at = lane + 128 * b - first_at
            inside = (at >= 0) & (at < WIN)
            at = jnp.where(inside, at, 0) + WIN * (c % 2)
            values = lane_gather(windows[:, 128 * (c // 2) : 128 * (c // 2) + 128], at)
            row.append(jnp.sum(jnp.where(inside, values, 0.0), axis=0, keepdims=True))
        span.append(row)
    for copy in l_copies:
        copy.wait()
    acc = jnp.zeros((RB, 128), F32)
    for c in range(3):
        for b in range(2):
            acc = acc + lblk[2 * c + b] * span[c][b]
    s2_send[...] = dot_exact(jnp.ones((8, 128), F32), acc, NT)[0:1]
    s2_recv[g] = s2_send[...]
    to_all(lambda peer: s2_send, s2_recv, s2_ss, s2_rs, False)
    halfway = jnp.sum(s2_recv[:, 0, :], axis=0, keepdims=True)
    halfway = jnp.broadcast_to(halfway, (8, RB))
    parts = []
    for c in range(3):
        at = jnp.where(lane < WIN, lane, lane - WIN) + first_at
        values = []
        for b in range(2):
            row = dot_exact(halfway, lblk[2 * c + b], NN)[0:1]
            values.append(
                lane_gather(jnp.broadcast_to(row, (n_dev, 128)), jnp.clip(at - 128 * b, 0, 127))
            )
        parts.append(jnp.where(at < 128, values[0], values[1]))
    s3_send[:, 0, 0:128] = jnp.where(lane < WIN, parts[0], parts[1])
    s3_send[:, 0, 128:256] = parts[2]
    s3_recv[d] = s3_send[d]
    to_all(lambda peer: s3_send.at[peer], s3_recv, s3_ss, s3_rs, True)
    total = jnp.sum(s3_recv[:, 0, :], axis=0, keepdims=True)
    correction = jnp.concatenate(
        [total[:, WIN * c : WIN * c + WIN] for c in range(3)] + [jnp.zeros((5, WIN), F32)], axis=0
    )
    ch, cl = split(correction)
    left = jnp.concatenate([ch, cl], axis=0)
    first = dot(left, pwh[...], NN)
    flat[0:8, :] = first[0:8] + first[8:16] + dot(ch, pwl[...], NN)
    for c in range(3):
        for r in range(ROWS):
            wi[c * ROWS + r : c * ROWS + r + 1, :] = flat[c : c + 1, 128 * r : 128 * r + 128]
    zi[...] = zi[...] + wi[...]
    for half in range(2):
        hi, lo = f_hi[8 * half : 8 * half + 8, :], f_lo[8 * half : 8 * half + 8, :]
        got = pick(
            lambda c, r: wi[c * ROWS + r : c * ROWS + r + 1, :], ROWS, hi, lo,
            [jnp.zeros((8, 128), F32)] * 3,
        )
        for c in range(3):
            at = slice(c * FROWS + 8 * half, c * FROWS + 8 * half + 8)
            zf[at, :] = zf[at, :] + got[c]
    gather_interior()
    gather_faces()
    operate(3, step_interior)
    step_faces()

    def last_interior():
        zi[...] = zi[...] + (ri[...] - wi[...]) * di[...]

    operate(4, last_interior)
    zf[...] = zf[...] + (rf[...] - wf[...]) * df[...]
    for q in range(4):
        hi, lo = v_hi[8 * q : 8 * q + 8, :], v_lo[8 * q : 8 * q + 8, :]
        rows = [slice(c * ROWS + 8 * q, c * ROWS + 8 * q + 8) for c in range(3)]
        got = pick(
            lambda c, r: zf[c * FROWS + r : c * FROWS + r + 1, :], FROWS, hi, lo,
            [zi[at, :] for at in rows],
        )
        for c in range(3):
            out_ref[rows[c], :] = got[c]


def solution(mesh):
    n_grp, n_dev = mesh.shape["grp"], mesh.shape["dev"]

    def local(rhs, nodes, coef, mass, faces, coarse, weights, matrix, chol):
        dma = pltpu.SemaphoreType.DMA

        def body(*refs):
            kernel(n_grp, n_dev, *refs)

        out = pl.pallas_call(
            body,
            name="two_level",
            out_shape=jax.ShapeDtypeStruct((96, 128), F32),
            in_specs=[pl.BlockSpec(memory_space=pltpu.HBM)] * 9,
            out_specs=pl.BlockSpec(memory_space=pltpu.VMEM),
            scratch_shapes=[
                *[pltpu.VMEM((3 * n, 128), F32) for n in (FROWS, ROWS) * 5],
                pltpu.VMEM((32, ELEM), I32),
                pltpu.VMEM((32, ELEM), I32),
                pltpu.VMEM((96, ELEM), F32),
                pltpu.VMEM((96, ELEM), F32),
                pltpu.VMEM((96, ELEM), F32),
                pltpu.VMEM((192, 96), BF16),
                pltpu.VMEM((NODES_PER * ELEM, 128), BF16),
                pltpu.VMEM((NODES_PER, FROWS + ROWS, ELEM), BF16),
                pltpu.VMEM((16, 128), I32),
                pltpu.VMEM((16, 128), I32),
                pltpu.VMEM((32, 128), I32),
                pltpu.VMEM((32, 128), I32),
                pltpu.VMEM((32, 128), I32),
                pltpu.VMEM((WIN, 4096), BF16),
                pltpu.VMEM((WIN, 4096), BF16),
                pltpu.VMEM((8, 4096), F32),
                pltpu.VMEM((27, 4, 128), I32),
                pltpu.VMEM((1, ELEM), F32),
                pltpu.VMEM((4, 512), I32),
                pltpu.VMEM((4, 4096), I32),
                pltpu.VMEM((4, 4096), F32),
                pltpu.VMEM((81, 81), F32),
                pltpu.VMEM((5, 4, 3, 4, 128), F32),
                pltpu.VMEM((5, 4, 3, 4, 128), F32),
                pltpu.VMEM((1, 256), F32),
                pltpu.VMEM((n_dev, 1, 256), F32),
                pltpu.VMEM((1, RB), F32),
                pltpu.VMEM((n_grp, 1, RB), F32),
                pltpu.VMEM((n_dev, 1, 256), F32),
                pltpu.VMEM((n_dev, 1, 256), F32),
                pltpu.VMEM((6, RB, 128), F32),
                dma((5, 4)), dma((5, 4)),
                dma((n_dev,)), dma((n_dev,)),
                dma((n_grp,)), dma((n_grp,)),
                dma((n_dev,)), dma((n_dev,)),
                dma((6,)),
                dma((8,)),
            ],
            compiler_params=pltpu.CompilerParams(
                collective_id=0, has_side_effects=True, vmem_limit_bytes=67_000_000
            ),
        )(
            rhs.reshape(96, 128), nodes.reshape(27, 4, 128), coef[0], mass.reshape(96, 128),
            faces[0, 0], coarse[0, 0], weights[0, 0], matrix, chol,
        )
        return out.reshape(1, 1, 3, 4096)

    return jax.shard_map(
        local,
        mesh=mesh,
        in_specs=(
            P("grp", "dev", None, None),
            P("grp", "dev", None, None),
            P("grp", "dev", None),
            P("grp", "dev", None, None),
            P("grp", "dev", None, None),
            P("grp", "dev", None, None),
            P("grp", "dev", None, None),
            P(),
            P("dev", None),
        ),
        out_specs=P("grp", "dev", None, None),
        check_vma=False,
    )
```

```python
import jax
import jax.numpy as jnp
from jax import lax
from jax.experimental import pallas as pl
from jax.experimental.pallas import tpu as pltpu
from jax.sharding import PartitionSpec as P

DAMPING = 0.6
MESH = pl.DeviceIdType.MESH
BF16 = jnp.bfloat16
F32 = jnp.float32
I32 = jnp.int32
NT = (((1,), (1,)), ((), ()))
NN = (((1,), (0,)), ((), ()))

ROWS = 32
FROWS = 16
NODES_PER = 27
ELEM = 512
CN = 1536
WIN = 64
RB = 288


def dot(a, b, dims):
    return lax.dot_general(a, b, dims, preferred_element_type=F32)


def dot_exact(a, b, dims):
    return lax.dot_general(
        a, b, dims, precision=lax.Precision.HIGHEST, preferred_element_type=F32
    )


def split(x):
    high = x.astype(BF16)
    low = (x - high.astype(F32)).astype(BF16)
    return high, low


def lane_gather(row, lanes):
    return jnp.take_along_axis(row, lanes, axis=1, mode="promise_in_bounds")


def pick(load_row, rows, hi, lo, start):
    got = list(start)
    fields = len(got)
    for r in range(rows):
        here = hi == r
        for c in range(fields):
            row = jnp.broadcast_to(load_row(c, r), hi.shape)
            got[c] = jnp.where(here, lane_gather(row, lo), got[c])
    return got


def kernel(
    n_grp, n_dev,
    rhs_hbm, nodes_hbm, coef_hbm, mass_hbm, face_hbm, cn_hbm, cw_hbm, em_hbm, chol_ref,
    out_ref,
    zf, zi, wf, wi, rf, ri, mf, mi, df, di,
    hi_i, lo_i, gath, p_hi, p_lo, m_hl, bn, oh,
    f_hi, f_lo, v_hi, v_lo, inv_t, pwh, pwl, pfh, pfl, lbh, lbl, win, flat,
    nodes_ref, coef_ref, face_ref, cn_ref, cw_ref, em_ref,
    send, recv, s1_send, s1_recv, s2_send, s2_recv, s3_send, s3_recv, lblk,
    send_sem, recv_sem, s1_ss, s1_rs, s2_ss, s2_rs, s3_ss, s3_rs, l_sem, in_sem,
):
    g = lax.axis_index("grp")
    d = lax.axis_index("dev")

    pairs = (
        (nodes_hbm, nodes_ref), (face_hbm, face_ref), (em_hbm, em_ref), (coef_hbm, coef_ref),
        (mass_hbm, mi), (rhs_hbm, ri), (cn_hbm, cn_ref), (cw_hbm, cw_ref),
    )
    loads = [pltpu.make_async_copy(a, b, in_sem.at[j]) for j, (a, b) in enumerate(pairs)]
    for load in loads:
        load.start()

    block0 = (3 * g) // 4
    block1 = lax.rem(block0 + 1, CN // 128)
    l_copies = []
    for c in range(3):
        for b, block in enumerate((block0, block1)):
            at = pl.multiple_of(CN * c + 128 * block, 128)
            copy = pltpu.make_async_copy(
                chol_ref.at[:, pl.ds(at, 128)], lblk.at[2 * c + b], l_sem.at[2 * c + b]
            )
            copy.start()
            l_copies.append(copy)

    barrier = pltpu.get_barrier_semaphore()
    for k in range(1, n_dev):
        pl.semaphore_signal(
            barrier, inc=1, device_id=(g, lax.rem(d + k, n_dev)), device_id_type=MESH
        )
    for k in range(1, n_grp):
        pl.semaphore_signal(
            barrier, inc=1, device_id=(lax.rem(g + k, n_grp), d), device_id_type=MESH
        )

    for load in loads:
        load.wait()
    for f in range(4):
        for r in range(4):
            face = face_ref[f : f + 1, 128 * r : 128 * r + 128]
            f_hi[4 * f + r : 4 * f + r + 1, :] = face >> 7
            f_lo[4 * f + r : 4 * f + r + 1, :] = face & 127

    def one_hot(index_row, count):
        at = jnp.broadcast_to(index_row, (count, index_row.shape[1]))
        number = lax.broadcasted_iota(I32, at.shape, 0)
        return jnp.where(at == number, 1.0, 0.0).astype(BF16)

    acc = jnp.zeros((64, 128), F32)
    for f in range(4):
        face = face_ref[f : f + 1, :]
        hot = one_hot(face >> 7, ROWS)
        slot = lax.broadcasted_iota(I32, (ROWS, ELEM), 1) + (512 * f + 1)
        a = jnp.concatenate(
            [(slot >> 6).astype(F32).astype(BF16) * hot, (slot & 63).astype(F32).astype(BF16) * hot],
            axis=0,
        )
        acc = acc + dot(a, one_hot(face & 127, 128), NT)
    inverse = (64.0 * acc[0:32] + acc[32:64]).astype(I32) - 1
    inv_t[...] = inverse
    v_hi[...] = inverse >> 7
    v_lo[...] = inverse & 127

    hi_i[...] = jnp.zeros((32, ELEM), I32)
    lo_i[...] = jnp.zeros((32, ELEM), I32)
    for i in range(NODES_PER):
        for k in range(4):
            index = nodes_ref[i, k : k + 1, :]
            hi_i[i : i + 1, 128 * k : 128 * k + 128] = index >> 7
            lo_i[i : i + 1, 128 * k : 128 * k + 128] = index & 127

    def renumber(v, carry):
        row = pl.multiple_of(8 * (v // 4), 8)
        lane = pl.multiple_of(128 * (v % 4), 128)
        at = (pl.ds(row, 8), pl.ds(lane, 128))
        hi, lo = hi_i[at], lo_i[at]
        slot = pick(lambda c, r: inv_t[r : r + 1, :], ROWS, hi, lo, [jnp.full((8, 128), -1, I32)])[0]
        hi_i[at] = jnp.where(slot >= 0, slot >> 7, hi + FROWS)
        lo_i[at] = jnp.where(slot >= 0, slot & 127, lo)
        return carry

    lax.fori_loop(0, 16, renumber, 0, unroll=4)

    def one_hot_faces(i, carry):
        oh[i, 0:FROWS] = one_hot(hi_i[pl.ds(i, 1), :], FROWS)
        return carry

    def one_hot_interior(i, carry):
        oh[i, FROWS:] = one_hot(hi_i[pl.ds(i, 1), :] - FROWS, ROWS)
        return carry

    lax.fori_loop(0, NODES_PER, one_hot_faces, 0)
    turned = lo_i[...].astype(F32).T
    number = lax.broadcasted_iota(I32, (ELEM, 128), 1).astype(F32)
    for i in range(NODES_PER):
        same = jnp.broadcast_to(turned[:, i : i + 1], (ELEM, 128)) == number
        bn[ELEM * i : ELEM * i + ELEM, :] = jnp.where(same, 1.0, 0.0).astype(BF16)

    def at_faces(source, target, idle):
        for half in range(2):
            hi, lo = f_hi[8 * half : 8 * half + 8, :], f_lo[8 * half : 8 * half + 8, :]
            got = pick(
                lambda c, r: source[c * ROWS + r : c * ROWS + r + 1, :], ROWS, hi, lo,
                [jnp.full((8, 128), idle, F32)] * 3,
            )
            for c in range(3):
                target[c * FROWS + 8 * half : c * FROWS + 8 * half + 8, :] = got[c]

    at_faces(mi, mf, 1.0)

    row_of = lax.broadcasted_iota(I32, (96, 81), 0)
    col_of = lax.broadcasted_iota(I32, (96, 81), 1)
    place = (col_of == 27 * (row_of // 32) + row_of % 32) & (row_of % 32 < 27)
    place = jnp.where(place, 1.0, 0.0)
    eye = lax.broadcasted_iota(I32, (81, 81), 0) == lax.broadcasted_iota(I32, (81, 81), 1)
    diag_row = jnp.sum(jnp.where(eye, em_ref[...], 0.0), axis=0, keepdims=True)
    main_diag = jnp.sum(place * diag_row, axis=1, keepdims=True)
    coef = coef_ref[...]

    def put_product(product):
        high = product.astype(BF16).astype(F32)
        p_hi[...] = high
        p_lo[...] = product - high

    def scatter(first, rows):
        columns = []
        for i in range(NODES_PER):
            hot = oh[i, first : first + rows]
            blocks = []
            for part in (p_hi, p_lo):
                for c in range(3):
                    row = part[c * 32 + i : c * 32 + i + 1, :]
                    value = jnp.broadcast_to(row, (rows, ELEM)).astype(BF16)
                    blocks.append(value * hot)
            columns.append(jnp.concatenate(blocks, axis=0))
        acc = dot(jnp.concatenate(columns, axis=1), bn[...], NN)
        return acc[0 : 3 * rows] + acc[3 * rows : 6 * rows]

    put_product(main_diag * coef)
    wf[...] = mf[...] + scatter(0, FROWS)

    pl.semaphore_wait(barrier, n_dev + n_grp - 2)

    up_g, down_g = lax.rem(g + 1, n_grp), lax.rem(g + n_grp - 1, n_grp)
    up_d, down_d = lax.rem(d + 1, n_dev), lax.rem(d + n_dev - 1, n_dev)
    partners = ((down_g, d), (up_g, d), (g, down_d), (g, up_d))

    def send_faces(k):
        for f in range(4):
            for c in range(3):
                send[k, f, c] = wf[c * FROWS + 4 * f : c * FROWS + 4 * f + 4, :]
        copies = []
        for f in range(4):
            copy = pltpu.make_async_remote_copy(
                src_ref=send.at[k, f],
                dst_ref=recv.at[k, f ^ 1],
                send_sem=send_sem.at[k, f],
                recv_sem=recv_sem.at[k, f ^ 1],
                device_id=partners[f],
                device_id_type=MESH,
            )
            copy.start()
            copies.append(copy)
        return copies

    def add_faces(k, copies):
        for copy in copies:
            copy.wait()
        for f in range(4):
            for c in range(3):
                at = slice(c * FROWS + 4 * f, c * FROWS + 4 * f + 4)
                wf[at, :] = wf[at, :] + recv[k, f, c]

    def gather(table, first, rows, fresh, unroll):
        def body(v, carry):
            row = pl.multiple_of(8 * (v // 4), 8)
            lane = pl.multiple_of(128 * (v % 4), 128)
            hi, lo = hi_i[pl.ds(row, 8), pl.ds(lane, 128)], lo_i[pl.ds(row, 8), pl.ds(lane, 128)]
            if fresh:
                start = [jnp.zeros((8, 128), F32)] * 3
            else:
                start = [gath[pl.ds(row + 32 * c, 8), pl.ds(lane, 128)] for c in range(3)]
            got = pick(
                lambda c, r: table[c * rows + r : c * rows + r + 1, :], rows, hi - first, lo, start
            )
            for c in range(3):
                gath[pl.ds(row + 32 * c, 8), pl.ds(lane, 128)] = got[c]
            return carry

        lax.fori_loop(0, 16, body, 0, unroll=unroll)

    def gather_interior():
        gather(zi, FROWS, ROWS, True, 8)

    def gather_faces():
        gather(zf, 0, FROWS, False, 16)

    def operate(k, interior):
        gh, gl = split(gath[...])
        both = dot(m_hl[...], gh, NN)
        product = both[0:96] + both[96:192] + dot(m_hl[0:96, :], gl, NN)
        put_product(product * coef)
        wf[...] = mf[...] * zf[...] + scatter(0, FROWS)
        copies = send_faces(k)
        wi[...] = mi[...] * zi[...] + scatter(FROWS, ROWS)
        interior()
        add_faces(k, copies)

    def step_interior():
        zi[...] = zi[...] + (ri[...] - wi[...]) * di[...]
        gather_interior()

    def step_faces():
        zf[...] = zf[...] + (rf[...] - wf[...]) * df[...]
        gather_faces()

    home = 6 * (n_dev * g + d)

    def fill(high_ref, low_ref, at, nodes, weights):
        shape = (WIN, nodes[0].shape[1])
        number = lax.broadcasted_iota(I32, shape, 0)
        total = jnp.zeros(shape, F32)
        for node, weight in zip(nodes, weights):
            rel = node - home
            rel = jnp.where(rel < 0, rel + CN, rel)
            hit = jnp.broadcast_to(rel, shape) == number
            total = total + jnp.where(hit, jnp.broadcast_to(weight, shape), 0.0)
        high_ref[:, at], low_ref[:, at] = split(total)

    def make_interpolation():
        def body(q, carry):
            at = pl.ds(pl.multiple_of(512 * q, 512), 512)
            fill(
                pwh, pwl, at,
                [cn_ref[j : j + 1, at] for j in range(4)], [cw_ref[j : j + 1, at] for j in range(4)],
            )
            return carry

        lax.fori_loop(0, 8, body, 0)

    def make_face_interpolation():
        for half in range(2):
            hi, lo = f_hi[8 * half : 8 * half + 8, :], f_lo[8 * half : 8 * half + 8, :]
            nodes = pick(
                lambda c, r: cn_ref[c : c + 1, 128 * r : 128 * r + 128], ROWS, hi, lo,
                [jnp.zeros((8, 128), I32)] * 4,
            )
            weights = pick(
                lambda c, r: cw_ref[c : c + 1, 128 * r : 128 * r + 128], ROWS, hi, lo,
                [jnp.zeros((8, 128), F32)] * 4,
            )
            for r in range(8):
                at = slice(128 * (8 * half + r), 128 * (8 * half + r) + 128)
                fill(
                    pfh, pfl, at, [n[r : r + 1] for n in nodes], [w[r : r + 1] for w in weights]
                )

    def restricted(values, high_ref, low_ref):
        rh, rl = split(values)
        both = dot(jnp.concatenate([rh, rl], axis=0), high_ref[...], NT)
        return both[0:8] + both[8:16] + dot(rh, low_ref[...], NT)

    def residual_interior():
        make_interpolation()
        for b in range(6):
            at = slice(128 * b, 128 * b + 128)
            lbh[:, at], lbl[:, at] = split(lblk[b])
        inside = v_hi[...] < 0
        for c in range(3):
            at = slice(c * ROWS, c * ROWS + ROWS)
            wi[at, :] = jnp.where(inside, ri[at, :] - wi[at, :], 0.0)
        flat[...] = jnp.zeros((8, 4096), F32)
        for c in range(3):
            for r in range(ROWS):
                flat[c : c + 1, 128 * r : 128 * r + 128] = wi[c * ROWS + r : c * ROWS + r + 1, :]
        win[...] = restricted(flat[...], pwh, pwl)

    copies = send_faces(0)
    lax.fori_loop(0, NODES_PER, one_hot_interior, 0)
    wi[...] = mi[...] + scatter(FROWS, ROWS)
    di[...] = DAMPING / wi[...]
    zi[...] = ri[...] * di[...]
    gather_interior()
    at_faces(ri, rf, 0.0)
    mh, ml = split(dot_exact(dot_exact(place, em_ref[...], NN), place, NT))
    m_hl[0:96, :] = mh
    m_hl[96:192, :] = ml
    add_faces(0, copies)
    df[...] = DAMPING / wf[...]
    zf[...] = rf[...] * df[...]
    gather_faces()
    def first_interior():
        step_interior()
        make_face_interpolation()
        for copy in l_copies:
            copy.wait()

    operate(1, first_interior)
    step_faces()
    operate(2, residual_interior)

    wf[...] = rf[...] - wf[...]
    flat[...] = jnp.zeros((8, 4096), F32)
    for c in range(3):
        for r in range(FROWS):
            flat[c : c + 1, 128 * r : 128 * r + 128] = wf[c * FROWS + r : c * FROWS + r + 1, :]
    window = win[...] + restricted(flat[:, 0 : 128 * FROWS], pfh, pfl)
    for c in range(3):
        s1_send[:, WIN * c : WIN * c + WIN] = window[c : c + 1]
    s1_send[:, 3 * WIN :] = jnp.zeros((1, 256 - 3 * WIN), F32)
    s1_recv[d] = s1_send[...]
    lane = lax.broadcasted_iota(I32, (n_dev, 128), 1)
    first_at = 6 * lax.broadcasted_iota(I32, (n_dev, 128), 0) + (96 * g - 128 * block0)

    def to_all(src, dst, send_sems, recv_sems, along_dev):
        me, count = (d, n_dev) if along_dev else (g, n_grp)
        copies = []
        for k in range(1, count):
            peer = lax.rem(me + k, count)
            copy = pltpu.make_async_remote_copy(
                src_ref=src(peer),
                dst_ref=dst.at[me],
                send_sem=send_sems.at[k],
                recv_sem=recv_sems.at[k],
                device_id=(g, peer) if along_dev else (peer, d),
                device_id_type=MESH,
            )
            copy.start()
            copies.append(copy)
        for copy in copies:
            copy.wait()

    to_all(lambda peer: s1_send, s1_recv, s1_ss, s1_rs, True)
    windows = s1_recv[:, 0, :]
    span = []
    for c in range(3):
        row = []
        for b in range(2):
            at = lane + 128 * b - first_at
            inside = (at >= 0) & (at < WIN)
            at = jnp.where(inside, at, 0) + WIN * (c % 2)
            values = lane_gather(windows[:, 128 * (c // 2) : 128 * (c // 2) + 128], at)
            row.append(jnp.sum(jnp.where(inside, values, 0.0), axis=0, keepdims=True))
        span.append(row)
    acc = jnp.zeros((RB, 128), F32)
    for c in range(3):
        for b in range(2):
            acc = acc + lblk[2 * c + b] * span[c][b]
    ah, al = split(acc)
    s2_send[...] = dot(jnp.ones((16, 256), BF16), jnp.concatenate([ah, al], axis=1), NT)[0:1]
    s2_recv[g] = s2_send[...]
    to_all(lambda peer: s2_send, s2_recv, s2_ss, s2_rs, False)
    halfway = jnp.sum(s2_recv[:, 0, :], axis=0, keepdims=True)
    hh, hl = split(jnp.broadcast_to(halfway, (8, RB)))
    both = dot(jnp.concatenate([hh, hl], axis=0), lbh[...], NN)
    partial = both[0:1] + both[8:9] + dot(hh, lbl[...], NN)[0:1]
    parts = []
    for c in range(3):
        at = jnp.where(lane < WIN, lane, lane - WIN) + first_at
        values = []
        for b in range(2):
            row = partial[:, 256 * c + 128 * b : 256 * c + 128 * b + 128]
            values.append(
                lane_gather(jnp.broadcast_to(row, (n_dev, 128)), jnp.clip(at - 128 * b, 0, 127))
            )
        parts.append(jnp.where(at < 128, values[0], values[1]))
    s3_send[:, 0, 0:128] = jnp.where(lane < WIN, parts[0], parts[1])
    s3_send[:, 0, 128:256] = parts[2]
    s3_recv[d] = s3_send[d]
    to_all(lambda peer: s3_send.at[peer], s3_recv, s3_ss, s3_rs, True)
    total = jnp.sum(s3_recv[:, 0, :], axis=0, keepdims=True)
    correction = jnp.concatenate(
        [total[:, WIN * c : WIN * c + WIN] for c in range(3)] + [jnp.zeros((5, WIN), F32)], axis=0
    )
    ch, cl = split(correction)
    left = jnp.concatenate([ch, cl], axis=0)
    for high, low, field, rows in ((pwh, pwl, zi, ROWS), (pfh, pfl, zf, FROWS)):
        both = dot(left, high[...], NN)
        flat[:, 0 : 128 * rows] = both[0:8] + both[8:16] + dot(ch, low[...], NN)
        for c in range(3):
            for r in range(rows):
                at = slice(c * rows + r, c * rows + r + 1)
                field[at, :] = field[at, :] + flat[c : c + 1, 128 * r : 128 * r + 128]
    gather_interior()
    gather_faces()
    operate(3, step_interior)
    step_faces()

    def last_interior():
        zi[...] = zi[...] + (ri[...] - wi[...]) * di[...]

    operate(4, last_interior)
    zf[...] = zf[...] + (rf[...] - wf[...]) * df[...]
    for q in range(4):
        hi, lo = v_hi[8 * q : 8 * q + 8, :], v_lo[8 * q : 8 * q + 8, :]
        rows = [slice(c * ROWS + 8 * q, c * ROWS + 8 * q + 8) for c in range(3)]
        got = pick(
            lambda c, r: zf[c * FROWS + r : c * FROWS + r + 1, :], FROWS, hi, lo,
            [zi[at, :] for at in rows],
        )
        for c in range(3):
            out_ref[rows[c], :] = got[c]


def solution(mesh):
    n_grp, n_dev = mesh.shape["grp"], mesh.shape["dev"]

    def local(rhs, nodes, coef, mass, faces, coarse, weights, matrix, chol):
        dma = pltpu.SemaphoreType.DMA

        def body(*refs):
            kernel(n_grp, n_dev, *refs)

        out = pl.pallas_call(
            body,
            name="two_level",
            out_shape=jax.ShapeDtypeStruct((96, 128), F32),
            in_specs=[pl.BlockSpec(memory_space=pltpu.HBM)] * 9,
            out_specs=pl.BlockSpec(memory_space=pltpu.VMEM),
            scratch_shapes=[
                *[pltpu.VMEM((3 * n, 128), F32) for n in (FROWS, ROWS) * 5],
                pltpu.VMEM((32, ELEM), I32),
                pltpu.VMEM((32, ELEM), I32),
                pltpu.VMEM((96, ELEM), F32),
                pltpu.VMEM((96, ELEM), F32),
                pltpu.VMEM((96, ELEM), F32),
                pltpu.VMEM((192, 96), BF16),
                pltpu.VMEM((NODES_PER * ELEM, 128), BF16),
                pltpu.VMEM((NODES_PER, FROWS + ROWS, ELEM), BF16),
                pltpu.VMEM((16, 128), I32),
                pltpu.VMEM((16, 128), I32),
                pltpu.VMEM((32, 128), I32),
                pltpu.VMEM((32, 128), I32),
                pltpu.VMEM((32, 128), I32),
                pltpu.VMEM((WIN, 4096), BF16),
                pltpu.VMEM((WIN, 4096), BF16),
                pltpu.VMEM((WIN, 128 * FROWS), BF16),
                pltpu.VMEM((WIN, 128 * FROWS), BF16),
                pltpu.VMEM((RB, 768), BF16),
                pltpu.VMEM((RB, 768), BF16),
                pltpu.VMEM((8, WIN), F32),
                pltpu.VMEM((8, 4096), F32),
                pltpu.VMEM((27, 4, 128), I32),
                pltpu.VMEM((1, ELEM), F32),
                pltpu.VMEM((4, 512), I32),
                pltpu.VMEM((4, 4096), I32),
                pltpu.VMEM((4, 4096), F32),
                pltpu.VMEM((81, 81), F32),
                pltpu.VMEM((5, 4, 3, 4, 128), F32),
                pltpu.VMEM((5, 4, 3, 4, 128), F32),
                pltpu.VMEM((1, 256), F32),
                pltpu.VMEM((n_dev, 1, 256), F32),
                pltpu.VMEM((1, RB), F32),
                pltpu.VMEM((n_grp, 1, RB), F32),
                pltpu.VMEM((n_dev, 1, 256), F32),
                pltpu.VMEM((n_dev, 1, 256), F32),
                pltpu.VMEM((6, RB, 128), F32),
                dma((5, 4)), dma((5, 4)),
                dma((n_dev,)), dma((n_dev,)),
                dma((n_grp,)), dma((n_grp,)),
                dma((n_dev,)), dma((n_dev,)),
                dma((6,)),
                dma((8,)),
            ],
            compiler_params=pltpu.CompilerParams(
                collective_id=0, has_side_effects=True, vmem_limit_bytes=67_000_000
            ),
        )(
            rhs.reshape(96, 128), nodes.reshape(27, 4, 128), coef[0], mass.reshape(96, 128),
            faces[0, 0], coarse[0, 0], weights[0, 0], matrix, chol,
        )
        return out.reshape(1, 1, 3, 4096)

    return jax.shard_map(
        local,
        mesh=mesh,
        in_specs=(
            P("grp", "dev", None, None),
            P("grp", "dev", None, None),
            P("grp", "dev", None),
            P("grp", "dev", None, None),
            P("grp", "dev", None, None),
            P("grp", "dev", None, None),
            P("grp", "dev", None, None),
            P(),
            P("dev", None),
        ),
        out_specs=P("grp", "dev", None, None),
        check_vma=False,
    )
```

```python
import jax
import jax.numpy as jnp
from jax import lax
from jax.experimental import pallas as pl
from jax.experimental.pallas import tpu as pltpu
from jax.sharding import PartitionSpec as P

DAMPING = 0.6
MESH = pl.DeviceIdType.MESH
BF16 = jnp.bfloat16
F32 = jnp.float32
I32 = jnp.int32
NT = (((1,), (1,)), ((), ()))
NN = (((1,), (0,)), ((), ()))

ROWS = 32
FROWS = 16
NODES_PER = 27
ELEM = 512
CN = 1536
WIN = 64
RB = 288


def dot(a, b, dims):
    return lax.dot_general(a, b, dims, preferred_element_type=F32)


def dot_exact(a, b, dims):
    return lax.dot_general(
        a, b, dims, precision=lax.Precision.HIGHEST, preferred_element_type=F32
    )


def split(x):
    high = x.astype(BF16)
    low = (x - high.astype(F32)).astype(BF16)
    return high, low


def lane_gather(row, lanes):
    return jnp.take_along_axis(row, lanes, axis=1, mode="promise_in_bounds")


def pick(load_row, rows, hi, lo, start):
    got = list(start)
    fields = len(got)
    for r in range(rows):
        here = hi == r
        for c in range(fields):
            row = jnp.broadcast_to(load_row(c, r), hi.shape)
            got[c] = jnp.where(here, lane_gather(row, lo), got[c])
    return got


def kernel(
    n_grp, n_dev,
    rhs_hbm, nodes_hbm, coef_hbm, mass_hbm, face_hbm, cn_hbm, cw_hbm, em_hbm, chol_ref,
    out_ref,
    zf, zi, wf, wi, rf, ri, mf, mi, df, di,
    hi_i, lo_i, gath, p_hi, p_lo, m_hl, bn, oh,
    f_hi, f_lo, v_hi, v_lo, inv_t, pwh, pwl, lbh, lbl, flat,
    nodes_ref, coef_ref, face_ref, cn_ref, cw_ref, em_ref,
    send, recv, s1_send, s1_recv, s2_send, s2_recv, s3_send, s3_recv, lblk,
    send_sem, recv_sem, s1_ss, s1_rs, s2_ss, s2_rs, s3_ss, s3_rs, l_sem, in_sem,
):
    g = lax.axis_index("grp")
    d = lax.axis_index("dev")

    pairs = (
        (nodes_hbm, nodes_ref), (face_hbm, face_ref), (em_hbm, em_ref), (coef_hbm, coef_ref),
        (mass_hbm, mi), (rhs_hbm, ri), (cn_hbm, cn_ref), (cw_hbm, cw_ref),
    )
    loads = [pltpu.make_async_copy(a, b, in_sem.at[j]) for j, (a, b) in enumerate(pairs)]
    for load in loads:
        load.start()

    block0 = (3 * g) // 4
    block1 = lax.rem(block0 + 1, CN // 128)
    l_copies = []
    for c in range(3):
        for b, block in enumerate((block0, block1)):
            at = pl.multiple_of(CN * c + 128 * block, 128)
            copy = pltpu.make_async_copy(
                chol_ref.at[:, pl.ds(at, 128)], lblk.at[2 * c + b], l_sem.at[2 * c + b]
            )
            copy.start()
            l_copies.append(copy)

    barrier = pltpu.get_barrier_semaphore()
    for k in range(1, n_dev):
        pl.semaphore_signal(
            barrier, inc=1, device_id=(g, lax.rem(d + k, n_dev)), device_id_type=MESH
        )
    for k in range(1, n_grp):
        pl.semaphore_signal(
            barrier, inc=1, device_id=(lax.rem(g + k, n_grp), d), device_id_type=MESH
        )

    for load in loads:
        load.wait()
    for f in range(4):
        for r in range(4):
            face = face_ref[f : f + 1, 128 * r : 128 * r + 128]
            f_hi[4 * f + r : 4 * f + r + 1, :] = face >> 7
            f_lo[4 * f + r : 4 * f + r + 1, :] = face & 127

    def one_hot(index_row, count):
        at = jnp.broadcast_to(index_row, (count, index_row.shape[1]))
        number = lax.broadcasted_iota(I32, at.shape, 0)
        return jnp.where(at == number, 1.0, 0.0).astype(BF16)

    acc = jnp.zeros((64, 128), F32)
    for f in range(4):
        face = face_ref[f : f + 1, :]
        hot = one_hot(face >> 7, ROWS)
        slot = lax.broadcasted_iota(I32, (ROWS, ELEM), 1) + (512 * f + 1)
        a = jnp.concatenate(
            [(slot >> 6).astype(F32).astype(BF16) * hot, (slot & 63).astype(F32).astype(BF16) * hot],
            axis=0,
        )
        acc = acc + dot(a, one_hot(face & 127, 128), NT)
    inverse = (64.0 * acc[0:32] + acc[32:64]).astype(I32) - 1
    inv_t[...] = inverse
    v_hi[...] = inverse >> 7
    v_lo[...] = inverse & 127

    hi_i[...] = jnp.zeros((32, ELEM), I32)
    lo_i[...] = jnp.zeros((32, ELEM), I32)
    for i in range(NODES_PER):
        for k in range(4):
            index = nodes_ref[i, k : k + 1, :]
            hi_i[i : i + 1, 128 * k : 128 * k + 128] = index >> 7
            lo_i[i : i + 1, 128 * k : 128 * k + 128] = index & 127

    def renumber(v, carry):
        row = pl.multiple_of(8 * (v // 4), 8)
        lane = pl.multiple_of(128 * (v % 4), 128)
        at = (pl.ds(row, 8), pl.ds(lane, 128))
        hi, lo = hi_i[at], lo_i[at]
        slot = pick(lambda c, r: inv_t[r : r + 1, :], ROWS, hi, lo, [jnp.full((8, 128), -1, I32)])[0]
        hi_i[at] = jnp.where(slot >= 0, slot >> 7, hi + FROWS)
        lo_i[at] = jnp.where(slot >= 0, slot & 127, lo)
        return carry

    lax.fori_loop(0, 16, renumber, 0, unroll=4)

    def one_hot_faces(i, carry):
        oh[i, 0:FROWS] = one_hot(hi_i[pl.ds(i, 1), :], FROWS)
        return carry

    def one_hot_interior(i, carry):
        oh[i, FROWS:] = one_hot(hi_i[pl.ds(i, 1), :] - FROWS, ROWS)
        return carry

    lax.fori_loop(0, NODES_PER, one_hot_faces, 0)
    turned = lo_i[...].astype(F32).T
    number = lax.broadcasted_iota(I32, (ELEM, 128), 1).astype(F32)
    for i in range(NODES_PER):
        same = jnp.broadcast_to(turned[:, i : i + 1], (ELEM, 128)) == number
        bn[ELEM * i : ELEM * i + ELEM, :] = jnp.where(same, 1.0, 0.0).astype(BF16)

    def at_faces(source, target, idle):
        for half in range(2):
            hi, lo = f_hi[8 * half : 8 * half + 8, :], f_lo[8 * half : 8 * half + 8, :]
            got = pick(
                lambda c, r: source[c * ROWS + r : c * ROWS + r + 1, :], ROWS, hi, lo,
                [jnp.full((8, 128), idle, F32)] * 3,
            )
            for c in range(3):
                target[c * FROWS + 8 * half : c * FROWS + 8 * half + 8, :] = got[c]

    at_faces(mi, mf, 1.0)

    row_of = lax.broadcasted_iota(I32, (96, 81), 0)
    col_of = lax.broadcasted_iota(I32, (96, 81), 1)
    place = (col_of == 27 * (row_of // 32) + row_of % 32) & (row_of % 32 < 27)
    place = jnp.where(place, 1.0, 0.0)
    eye = lax.broadcasted_iota(I32, (81, 81), 0) == lax.broadcasted_iota(I32, (81, 81), 1)
    diag_row = jnp.sum(jnp.where(eye, em_ref[...], 0.0), axis=0, keepdims=True)
    main_diag = jnp.sum(place * diag_row, axis=1, keepdims=True)
    coef = coef_ref[...]

    def put_product(product):
        high = product.astype(BF16).astype(F32)
        p_hi[...] = high
        p_lo[...] = product - high

    def scatter(first, rows):
        columns = []
        for i in range(NODES_PER):
            hot = oh[i, first : first + rows]
            blocks = []
            for part in (p_hi, p_lo):
                for c in range(3):
                    row = part[c * 32 + i : c * 32 + i + 1, :]
                    value = jnp.broadcast_to(row, (rows, ELEM)).astype(BF16)
                    blocks.append(value * hot)
            columns.append(jnp.concatenate(blocks, axis=0))
        acc = dot(jnp.concatenate(columns, axis=1), bn[...], NN)
        return acc[0 : 3 * rows] + acc[3 * rows : 6 * rows]

    up_g, down_g = lax.rem(g + 1, n_grp), lax.rem(g + n_grp - 1, n_grp)
    up_d, down_d = lax.rem(d + 1, n_dev), lax.rem(d + n_dev - 1, n_dev)
    partners = ((down_g, d), (up_g, d), (g, down_d), (g, up_d))

    def send_faces(k):
        for f in range(4):
            for c in range(3):
                send[k, f, c] = wf[c * FROWS + 4 * f : c * FROWS + 4 * f + 4, :]
        copies = []
        for f in range(4):
            copy = pltpu.make_async_remote_copy(
                src_ref=send.at[k, f],
                dst_ref=recv.at[k, f ^ 1],
                send_sem=send_sem.at[k, f],
                recv_sem=recv_sem.at[k, f ^ 1],
                device_id=partners[f],
                device_id_type=MESH,
            )
            copy.start()
            copies.append(copy)
        return copies

    def add_faces(k, copies):
        for copy in copies:
            copy.wait()
        for f in range(4):
            for c in range(3):
                at = slice(c * FROWS + 4 * f, c * FROWS + 4 * f + 4)
                wf[at, :] = wf[at, :] + recv[k, f, c]

    def gather(table, first, rows, fresh, unroll):
        def body(v, carry):
            row = pl.multiple_of(8 * (v // 4), 8)
            lane = pl.multiple_of(128 * (v % 4), 128)
            hi, lo = hi_i[pl.ds(row, 8), pl.ds(lane, 128)], lo_i[pl.ds(row, 8), pl.ds(lane, 128)]
            if fresh:
                start = [jnp.zeros((8, 128), F32)] * 3
            else:
                start = [gath[pl.ds(row + 32 * c, 8), pl.ds(lane, 128)] for c in range(3)]
            got = pick(
                lambda c, r: table[c * rows + r : c * rows + r + 1, :], rows, hi - first, lo, start
            )
            for c in range(3):
                gath[pl.ds(row + 32 * c, 8), pl.ds(lane, 128)] = got[c]
            return carry

        lax.fori_loop(0, 16, body, 0, unroll=unroll)

    def gather_interior():
        gather(zi, FROWS, ROWS, True, 8)

    def gather_faces():
        gather(zf, 0, FROWS, False, 8)

    home = 6 * (n_dev * g + d)

    def fill(high_ref, low_ref, at, nodes, weights):
        shape = (WIN, nodes[0].shape[1])
        number = lax.broadcasted_iota(I32, shape, 0)
        total = jnp.zeros(shape, F32)
        for node, weight in zip(nodes, weights):
            rel = node - home
            rel = jnp.where(rel < 0, rel + CN, rel)
            hit = jnp.broadcast_to(rel, shape) == number
            total = total + jnp.where(hit, jnp.broadcast_to(weight, shape), 0.0)
        high_ref[:, at], low_ref[:, at] = split(total)

    def make_interpolation():
        def body(q, carry):
            at = pl.ds(pl.multiple_of(512 * q, 512), 512)
            fill(
                pwh, pwl, at,
                [cn_ref[j : j + 1, at] for j in range(4)], [cw_ref[j : j + 1, at] for j in range(4)],
            )
            return carry

        lax.fori_loop(0, 8, body, 0)

    def restricted(values, high_ref, low_ref):
        rh, rl = split(values)
        both = dot(jnp.concatenate([rh, rl], axis=0), high_ref[...], NT)
        return both[0:8] + both[8:16] + dot(rh, low_ref[...], NT)

    def coarse_correction():
        for q in range(4):
            hi, lo = v_hi[8 * q : 8 * q + 8, :], v_lo[8 * q : 8 * q + 8, :]
            rows = [slice(c * ROWS + 8 * q, c * ROWS + 8 * q + 8) for c in range(3)]
            got = pick(
                lambda c, r: wf[c * FROWS + r : c * FROWS + r + 1, :], FROWS, hi, lo,
                [wi[at, :] for at in rows],
            )
            for c in range(3):
                wi[rows[c], :] = got[c]
        for c in range(3):
            for r in range(ROWS):
                flat[c : c + 1, 128 * r : 128 * r + 128] = wi[c * ROWS + r : c * ROWS + r + 1, :]
        window = restricted(flat[...], pwh, pwl)
        for c in range(3):
            s1_send[:, WIN * c : WIN * c + WIN] = window[c : c + 1]
        s1_send[:, 3 * WIN :] = jnp.zeros((1, 256 - 3 * WIN), F32)
        s1_recv[d] = s1_send[...]
        lane = lax.broadcasted_iota(I32, (n_dev, 128), 1)
        first_at = 6 * lax.broadcasted_iota(I32, (n_dev, 128), 0) + (96 * g - 128 * block0)

        def to_all(src, dst, send_sems, recv_sems, along_dev, cover=None):
            me, count = (d, n_dev) if along_dev else (g, n_grp)
            copies = []
            for k in range(1, count):
                peer = lax.rem(me + k, count)
                copy = pltpu.make_async_remote_copy(
                    src_ref=src(peer),
                    dst_ref=dst.at[me],
                    send_sem=send_sems.at[k],
                    recv_sem=recv_sems.at[k],
                    device_id=(g, peer) if along_dev else (peer, d),
                    device_id_type=MESH,
                )
                copy.start()
                copies.append(copy)
            if cover is not None:
                cover()
            for copy in copies:
                copy.wait()

        def split_factor():
            for copy in l_copies:
                copy.wait()
            for b in range(6):
                at = slice(128 * b, 128 * b + 128)
                lbh[:, at], lbl[:, at] = split(lblk[b])

        to_all(lambda peer: s1_send, s1_recv, s1_ss, s1_rs, True, split_factor)
        windows = s1_recv[:, 0, :]
        span = []
        for c in range(3):
            row = []
            for b in range(2):
                at = lane + 128 * b - first_at
                inside = (at >= 0) & (at < WIN)
                at = jnp.where(inside, at, 0) + WIN * (c % 2)
                values = lane_gather(windows[:, 128 * (c // 2) : 128 * (c // 2) + 128], at)
                row.append(jnp.sum(jnp.where(inside, values, 0.0), axis=0, keepdims=True))
            span.append(row)
        acc = jnp.zeros((RB, 128), F32)
        for c in range(3):
            for b in range(2):
                acc = acc + lblk[2 * c + b] * span[c][b]
        ah, al = split(acc)
        s2_send[...] = dot(jnp.ones((16, 256), BF16), jnp.concatenate([ah, al], axis=1), NT)[0:1]
        s2_recv[g] = s2_send[...]
        to_all(lambda peer: s2_send, s2_recv, s2_ss, s2_rs, False)
        halfway = jnp.sum(s2_recv[:, 0, :], axis=0, keepdims=True)
        hh, hl = split(jnp.broadcast_to(halfway, (8, RB)))
        both = dot(jnp.concatenate([hh, hl], axis=0), lbh[...], NN)
        partial = both[0:1] + both[8:9] + dot(hh, lbl[...], NN)[0:1]
        parts = []
        for c in range(3):
            at = jnp.where(lane < WIN, lane, lane - WIN) + first_at
            values = []
            for b in range(2):
                row = partial[:, 256 * c + 128 * b : 256 * c + 128 * b + 128]
                values.append(
                    lane_gather(jnp.broadcast_to(row, (n_dev, 128)), jnp.clip(at - 128 * b, 0, 127))
                )
            parts.append(jnp.where(at < 128, values[0], values[1]))
        s3_send[:, 0, 0:128] = jnp.where(lane < WIN, parts[0], parts[1])
        s3_send[:, 0, 128:256] = parts[2]
        s3_recv[d] = s3_send[d]
        to_all(lambda peer: s3_send.at[peer], s3_recv, s3_ss, s3_rs, True)
        total = jnp.sum(s3_recv[:, 0, :], axis=0, keepdims=True)
        correction = jnp.concatenate(
            [total[:, WIN * c : WIN * c + WIN] for c in range(3)] + [jnp.zeros((5, WIN), F32)], axis=0
        )
        ch, cl = split(correction)
        left = jnp.concatenate([ch, cl], axis=0)
        both = dot(left, pwh[...], NN)
        flat[...] = both[0:8] + both[8:16] + dot(ch, pwl[...], NN)
        for c in range(3):
            for r in range(ROWS):
                wi[c * ROWS + r : c * ROWS + r + 1, :] = flat[c : c + 1, 128 * r : 128 * r + 128]
        zi[...] = zi[...] + wi[...]
        for half in range(2):
            hi, lo = f_hi[8 * half : 8 * half + 8, :], f_lo[8 * half : 8 * half + 8, :]
            got = pick(
                lambda c, r: wi[c * ROWS + r : c * ROWS + r + 1, :], ROWS, hi, lo,
                [jnp.zeros((8, 128), F32)] * 3,
            )
            for c in range(3):
                at = slice(c * FROWS + 8 * half, c * FROWS + 8 * half + 8)
                zf[at, :] = zf[at, :] + got[c]
        gather_interior()

    def apply(k, carry):
        @pl.when(k == 0)
        def _():
            put_product(main_diag * coef)

        @pl.when(k > 0)
        def _():
            gh, gl = split(gath[...])
            both = dot(m_hl[...], gh, NN)
            product = both[0:96] + both[96:192] + dot(m_hl[0:96, :], gl, NN)
            put_product(product * coef)

        wf[...] = mf[...] * zf[...] + scatter(0, FROWS)

        @pl.when(k == 0)
        def _():
            pl.semaphore_wait(barrier, n_dev + n_grp - 2)

        copies = send_faces(k)

        @pl.when(k == 0)
        def _():
            lax.fori_loop(0, NODES_PER, one_hot_interior, 0)

        wi[...] = mi[...] * zi[...] + scatter(FROWS, ROWS)

        @pl.when(k == 0)
        def _():
            di[...] = DAMPING / wi[...]
            zi[...] = ri[...] * di[...]
            at_faces(ri, rf, 0.0)
            mh, ml = split(dot_exact(dot_exact(place, em_ref[...], NN), place, NT))
            m_hl[0:96, :] = mh
            m_hl[96:192, :] = ml

        @pl.when(k == 2)
        def _():
            wi[...] = ri[...] - wi[...]
            flat[...] = jnp.zeros((8, 4096), F32)
            make_interpolation()

        @pl.when((k != 0) & (k != 2))
        def _():
            zi[...] = zi[...] + (ri[...] - wi[...]) * di[...]

        @pl.when((k != 2) & (k != 4))
        def _():
            gather_interior()

        add_faces(k, copies)

        @pl.when(k == 0)
        def _():
            df[...] = DAMPING / wf[...]
            zf[...] = rf[...] * df[...]

        @pl.when(k == 2)
        def _():
            wf[...] = rf[...] - wf[...]
            coarse_correction()

        @pl.when((k != 0) & (k != 2))
        def _():
            zf[...] = zf[...] + (rf[...] - wf[...]) * df[...]

        @pl.when(k != 4)
        def _():
            gather_faces()

        return carry

    zf[...] = jnp.ones((3 * FROWS, 128), F32)
    zi[...] = jnp.ones((3 * ROWS, 128), F32)
    lax.fori_loop(0, 5, apply, 0)
    for q in range(4):
        hi, lo = v_hi[8 * q : 8 * q + 8, :], v_lo[8 * q : 8 * q + 8, :]
        rows = [slice(c * ROWS + 8 * q, c * ROWS + 8 * q + 8) for c in range(3)]
        got = pick(
            lambda c, r: zf[c * FROWS + r : c * FROWS + r + 1, :], FROWS, hi, lo,
            [zi[at, :] for at in rows],
        )
        for c in range(3):
            out_ref[rows[c], :] = got[c]


def solution(mesh):
    n_grp, n_dev = mesh.shape["grp"], mesh.shape["dev"]

    def local(rhs, nodes, coef, mass, faces, coarse, weights, matrix, chol):
        dma = pltpu.SemaphoreType.DMA

        def body(*refs):
            kernel(n_grp, n_dev, *refs)

        out = pl.pallas_call(
            body,
            name="two_level",
            out_shape=jax.ShapeDtypeStruct((96, 128), F32),
            in_specs=[pl.BlockSpec(memory_space=pltpu.HBM)] * 9,
            out_specs=pl.BlockSpec(memory_space=pltpu.VMEM),
            scratch_shapes=[
                *[pltpu.VMEM((3 * n, 128), F32) for n in (FROWS, ROWS) * 5],
                pltpu.VMEM((32, ELEM), I32),
                pltpu.VMEM((32, ELEM), I32),
                pltpu.VMEM((96, ELEM), F32),
                pltpu.VMEM((96, ELEM), F32),
                pltpu.VMEM((96, ELEM), F32),
                pltpu.VMEM((192, 96), BF16),
                pltpu.VMEM((NODES_PER * ELEM, 128), BF16),
                pltpu.VMEM((NODES_PER, FROWS + ROWS, ELEM), BF16),
                pltpu.VMEM((16, 128), I32),
                pltpu.VMEM((16, 128), I32),
                pltpu.VMEM((32, 128), I32),
                pltpu.VMEM((32, 128), I32),
                pltpu.VMEM((32, 128), I32),
                pltpu.VMEM((WIN, 4096), BF16),
                pltpu.VMEM((WIN, 4096), BF16),
                pltpu.VMEM((RB, 768), BF16),
                pltpu.VMEM((RB, 768), BF16),
                pltpu.VMEM((8, 4096), F32),
                pltpu.VMEM((27, 4, 128), I32),
                pltpu.VMEM((1, ELEM), F32),
                pltpu.VMEM((4, 512), I32),
                pltpu.VMEM((4, 4096), I32),
                pltpu.VMEM((4, 4096), F32),
                pltpu.VMEM((81, 81), F32),
                pltpu.VMEM((5, 4, 3, 4, 128), F32),
                pltpu.VMEM((5, 4, 3, 4, 128), F32),
                pltpu.VMEM((1, 256), F32),
                pltpu.VMEM((n_dev, 1, 256), F32),
                pltpu.VMEM((1, RB), F32),
                pltpu.VMEM((n_grp, 1, RB), F32),
                pltpu.VMEM((n_dev, 1, 256), F32),
                pltpu.VMEM((n_dev, 1, 256), F32),
                pltpu.VMEM((6, RB, 128), F32),
                dma((5, 4)), dma((5, 4)),
                dma((n_dev,)), dma((n_dev,)),
                dma((n_grp,)), dma((n_grp,)),
                dma((n_dev,)), dma((n_dev,)),
                dma((6,)),
                dma((8,)),
            ],
            compiler_params=pltpu.CompilerParams(
                collective_id=0, has_side_effects=True, vmem_limit_bytes=67_000_000
            ),
        )(
            rhs.reshape(96, 128), nodes.reshape(27, 4, 128), coef[0], mass.reshape(96, 128),
            faces[0, 0], coarse[0, 0], weights[0, 0], matrix, chol,
        )
        return out.reshape(1, 1, 3, 4096)

    return jax.shard_map(
        local,
        mesh=mesh,
        in_specs=(
            P("grp", "dev", None, None),
            P("grp", "dev", None, None),
            P("grp", "dev", None),
            P("grp", "dev", None, None),
            P("grp", "dev", None, None),
            P("grp", "dev", None, None),
            P("grp", "dev", None, None),
            P(),
            P("dev", None),
        ),
        out_specs=P("grp", "dev", None, None),
        check_vma=False,
    )
```

```python
import jax
import jax.numpy as jnp
from jax import lax
from jax.experimental import pallas as pl
from jax.experimental.pallas import tpu as pltpu
from jax.sharding import PartitionSpec as P

DAMPING = 0.6
MESH = pl.DeviceIdType.MESH
BF16 = jnp.bfloat16
F32 = jnp.float32
I32 = jnp.int32
NT = (((1,), (1,)), ((), ()))
NN = (((1,), (0,)), ((), ()))

ROWS = 32
FROWS = 16
NODES_PER = 27
ELEM = 512
CN = 1536
WIN = 64
RB = 288


def dot(a, b, dims):
    return lax.dot_general(a, b, dims, preferred_element_type=F32)


def dot_exact(a, b, dims):
    return lax.dot_general(
        a, b, dims, precision=lax.Precision.HIGHEST, preferred_element_type=F32
    )


def split(x):
    high = x.astype(BF16)
    low = (x - high.astype(F32)).astype(BF16)
    return high, low


def lane_gather(row, lanes):
    return jnp.take_along_axis(row, lanes, axis=1, mode="promise_in_bounds")


def pick(load_row, rows, hi, lo, start):
    got = list(start)
    fields = len(got)
    for r in range(rows):
        here = hi == r
        for c in range(fields):
            row = jnp.broadcast_to(load_row(c, r), hi.shape)
            got[c] = jnp.where(here, lane_gather(row, lo), got[c])
    return got


def kernel(
    n_grp, n_dev,
    rhs_hbm, nodes_hbm, coef_hbm, mass_hbm, face_hbm, cn_hbm, cw_hbm, em_hbm, chol_ref,
    out_ref,
    zf, zi, wf, wi, rf, ri, mf, mi, df, di,
    hi_i, lo_i, gath, p_hi, p_lo, m_hl, bn, hot_g, hot_d, oh,
    f_hi, f_lo, v_hi, v_lo, inv_t, pwh, pwl, lbh, lbl, flat,
    nodes_ref, coef_ref, face_ref, cn_ref, cw_ref, em_ref,
    send, recv, s1_send, s1_recv, s2_send, s2_recv, s3_send, s3_recv, lblk,
    send_sem, recv_sem, s1_ss, s1_rs, s2_ss, s2_rs, s3_ss, s3_rs, l_sem, in_sem,
):
    g = lax.axis_index("grp")
    d = lax.axis_index("dev")

    pairs = (
        (nodes_hbm, nodes_ref), (face_hbm, face_ref), (em_hbm, em_ref), (coef_hbm, coef_ref),
        (mass_hbm, mi), (rhs_hbm, ri), (cn_hbm, cn_ref), (cw_hbm, cw_ref),
    )
    loads = [pltpu.make_async_copy(a, b, in_sem.at[j]) for j, (a, b) in enumerate(pairs)]
    for load in loads:
        load.start()

    block0 = (3 * g) // 4
    block1 = lax.rem(block0 + 1, CN // 128)
    l_copies = []
    for c in range(3):
        for b, block in enumerate((block0, block1)):
            at = pl.multiple_of(CN * c + 128 * block, 128)
            copy = pltpu.make_async_copy(
                chol_ref.at[:, pl.ds(at, 128)], lblk.at[2 * c + b], l_sem.at[2 * c + b]
            )
            copy.start()
            l_copies.append(copy)

    barrier = pltpu.get_barrier_semaphore()
    for k in range(1, n_dev):
        pl.semaphore_signal(
            barrier, inc=1, device_id=(g, lax.rem(d + k, n_dev)), device_id_type=MESH
        )
    for k in range(1, n_grp):
        pl.semaphore_signal(
            barrier, inc=1, device_id=(lax.rem(g + k, n_grp), d), device_id_type=MESH
        )

    for load in loads:
        load.wait()
    for f in range(4):
        for r in range(4):
            face = face_ref[f : f + 1, 128 * r : 128 * r + 128]
            f_hi[4 * f + r : 4 * f + r + 1, :] = face >> 7
            f_lo[4 * f + r : 4 * f + r + 1, :] = face & 127

    def one_hot(index_row, count):
        at = jnp.broadcast_to(index_row, (count, index_row.shape[1]))
        number = lax.broadcasted_iota(I32, at.shape, 0)
        return jnp.where(at == number, 1.0, 0.0).astype(BF16)

    acc = jnp.zeros((64, 128), F32)
    for f in range(4):
        face = face_ref[f : f + 1, :]
        hot = one_hot(face >> 7, ROWS)
        slot = lax.broadcasted_iota(I32, (ROWS, ELEM), 1) + (512 * f + 1)
        a = jnp.concatenate(
            [(slot >> 6).astype(F32).astype(BF16) * hot, (slot & 63).astype(F32).astype(BF16) * hot],
            axis=0,
        )
        acc = acc + dot(a, one_hot(face & 127, 128), NT)
    inverse = (64.0 * acc[0:32] + acc[32:64]).astype(I32) - 1
    inv_t[...] = inverse
    v_hi[...] = inverse >> 7
    v_lo[...] = inverse & 127

    hi_i[...] = jnp.zeros((32, ELEM), I32)
    lo_i[...] = jnp.zeros((32, ELEM), I32)
    for i in range(NODES_PER):
        for k in range(4):
            index = nodes_ref[i, k : k + 1, :]
            hi_i[i : i + 1, 128 * k : 128 * k + 128] = index >> 7
            lo_i[i : i + 1, 128 * k : 128 * k + 128] = index & 127

    def renumber(v, carry):
        row = pl.multiple_of(8 * (v // 4), 8)
        lane = pl.multiple_of(128 * (v % 4), 128)
        at = (pl.ds(row, 8), pl.ds(lane, 128))
        hi, lo = hi_i[at], lo_i[at]
        slot = pick(lambda c, r: inv_t[r : r + 1, :], ROWS, hi, lo, [jnp.full((8, 128), -1, I32)])[0]
        hi_i[at] = jnp.where(slot >= 0, slot >> 7, hi + FROWS)
        lo_i[at] = jnp.where(slot >= 0, slot & 127, lo)
        return carry

    lax.fori_loop(0, 16, renumber, 0, unroll=4)

    twice = lax.broadcasted_iota(I32, (16, ELEM), 0) % 8

    def one_hot_faces(i, carry):
        at = jnp.broadcast_to(hi_i[pl.ds(i, 1), :], (16, ELEM))
        hot_g[i] = jnp.where(at == twice, 1.0, 0.0).astype(BF16)
        hot_d[i] = jnp.where(at == twice + 8, 1.0, 0.0).astype(BF16)
        return carry

    def one_hot_interior(i, carry):
        oh[i] = one_hot(hi_i[pl.ds(i, 1), :] - FROWS, ROWS)
        return carry

    lax.fori_loop(0, NODES_PER, one_hot_faces, 0)
    turned = lo_i[...].astype(F32).T
    number = lax.broadcasted_iota(I32, (ELEM, 128), 1).astype(F32)
    for i in range(NODES_PER):
        same = jnp.broadcast_to(turned[:, i : i + 1], (ELEM, 128)) == number
        bn[ELEM * i : ELEM * i + ELEM, :] = jnp.where(same, 1.0, 0.0).astype(BF16)

    def at_faces(source, target, idle):
        for half in range(2):
            hi, lo = f_hi[8 * half : 8 * half + 8, :], f_lo[8 * half : 8 * half + 8, :]
            got = pick(
                lambda c, r: source[c * ROWS + r : c * ROWS + r + 1, :], ROWS, hi, lo,
                [jnp.full((8, 128), idle, F32)] * 3,
            )
            for c in range(3):
                target[c * FROWS + 8 * half : c * FROWS + 8 * half + 8, :] = got[c]

    at_faces(mi, mf, 1.0)

    row_of = lax.broadcasted_iota(I32, (96, 81), 0)
    col_of = lax.broadcasted_iota(I32, (96, 81), 1)
    place = (col_of == 27 * (row_of // 32) + row_of % 32) & (row_of % 32 < 27)
    place = jnp.where(place, 1.0, 0.0)
    eye = lax.broadcasted_iota(I32, (81, 81), 0) == lax.broadcasted_iota(I32, (81, 81), 1)
    diag_row = jnp.sum(jnp.where(eye, em_ref[...], 0.0), axis=0, keepdims=True)
    main_diag = jnp.sum(place * diag_row, axis=1, keepdims=True)
    coef = coef_ref[...]

    def put_product(product):
        high = product.astype(BF16).astype(F32)
        p_hi[...] = high
        p_lo[...] = product - high

    def scatter(rows):
        columns = []
        for i in range(NODES_PER):
            hot = oh[i]
            blocks = []
            for part in (p_hi, p_lo):
                for c in range(3):
                    row = part[c * 32 + i : c * 32 + i + 1, :]
                    value = jnp.broadcast_to(row, (rows, ELEM)).astype(BF16)
                    blocks.append(value * hot)
            columns.append(jnp.concatenate(blocks, axis=0))
        acc = dot(jnp.concatenate(columns, axis=1), bn[...], NN)
        return acc[0 : 3 * rows] + acc[3 * rows : 6 * rows]

    def scatter_faces(hots):
        columns = []
        for i in range(NODES_PER):
            hot = hots[i]
            blocks = []
            for c in range(3):
                at = slice(c * 32 + i, c * 32 + i + 1)
                value = jnp.concatenate(
                    [jnp.broadcast_to(p_hi[at, :], (8, ELEM)), jnp.broadcast_to(p_lo[at, :], (8, ELEM))],
                    axis=0,
                )
                blocks.append(value.astype(BF16) * hot)
            columns.append(jnp.concatenate(blocks, axis=0))
        acc = dot(jnp.concatenate(columns, axis=1), bn[...], NN)
        return [acc[16 * c : 16 * c + 8] + acc[16 * c + 8 : 16 * c + 16] for c in range(3)]

    up_g, down_g = lax.rem(g + 1, n_grp), lax.rem(g + n_grp - 1, n_grp)
    up_d, down_d = lax.rem(d + 1, n_dev), lax.rem(d + n_dev - 1, n_dev)
    partners = ((down_g, d), (up_g, d), (g, down_d), (g, up_d))

    def send_faces(k, faces):
        for f in faces:
            for c in range(3):
                send[k, f, c] = wf[c * FROWS + 4 * f : c * FROWS + 4 * f + 4, :]
        copies = []
        for f in faces:
            copy = pltpu.make_async_remote_copy(
                src_ref=send.at[k, f],
                dst_ref=recv.at[k, f ^ 1],
                send_sem=send_sem.at[k, f],
                recv_sem=recv_sem.at[k, f ^ 1],
                device_id=partners[f],
                device_id_type=MESH,
            )
            copy.start()
            copies.append(copy)
        return copies

    def add_faces(k, faces, copies):
        for copy in copies:
            copy.wait()
        for f in faces:
            for c in range(3):
                at = slice(c * FROWS + 4 * f, c * FROWS + 4 * f + 4)
                wf[at, :] = wf[at, :] + recv[k, f, c]

    def gather(table, stride, base, first, rows, fresh, unroll):
        def body(v, carry):
            row = pl.multiple_of(8 * (v // 4), 8)
            lane = pl.multiple_of(128 * (v % 4), 128)
            hi, lo = hi_i[pl.ds(row, 8), pl.ds(lane, 128)], lo_i[pl.ds(row, 8), pl.ds(lane, 128)]
            if fresh:
                start = [jnp.zeros((8, 128), F32)] * 3
            else:
                start = [gath[pl.ds(row + 32 * c, 8), pl.ds(lane, 128)] for c in range(3)]
            got = pick(
                lambda c, r: table[c * stride + base + r : c * stride + base + r + 1, :],
                rows, hi - first, lo, start,
            )
            for c in range(3):
                gath[pl.ds(row + 32 * c, 8), pl.ds(lane, 128)] = got[c]
            return carry

        lax.fori_loop(0, 16, body, 0, unroll=unroll)

    def gather_interior():
        gather(zi, ROWS, 0, FROWS, ROWS, True, 8)

    def gather_faces(base):
        gather(zf, FROWS, base, base, 8, False, 8)

    def face_rows(base):
        return [slice(c * FROWS + base, c * FROWS + base + 8) for c in range(3)]

    def step_faces(k, base):
        @pl.when(k == 0)
        def _():
            for at in face_rows(base):
                df[at, :] = DAMPING / wf[at, :]
                zf[at, :] = rf[at, :] * df[at, :]

        @pl.when((k != 0) & (k != 2))
        def _():
            for at in face_rows(base):
                zf[at, :] = zf[at, :] + (rf[at, :] - wf[at, :]) * df[at, :]

    home = 6 * (n_dev * g + d)

    def fill(high_ref, low_ref, at, nodes, weights):
        shape = (WIN, nodes[0].shape[1])
        number = lax.broadcasted_iota(I32, shape, 0)
        total = jnp.zeros(shape, F32)
        for node, weight in zip(nodes, weights):
            rel = node - home
            rel = jnp.where(rel < 0, rel + CN, rel)
            hit = jnp.broadcast_to(rel, shape) == number
            total = total + jnp.where(hit, jnp.broadcast_to(weight, shape), 0.0)
        high_ref[:, at], low_ref[:, at] = split(total)

    def make_interpolation():
        def body(q, carry):
            at = pl.ds(pl.multiple_of(512 * q, 512), 512)
            fill(
                pwh, pwl, at,
                [cn_ref[j : j + 1, at] for j in range(4)], [cw_ref[j : j + 1, at] for j in range(4)],
            )
            return carry

        lax.fori_loop(0, 8, body, 0)

    def restricted(values, high_ref, low_ref):
        rh, rl = split(values)
        both = dot(jnp.concatenate([rh, rl], axis=0), high_ref[...], NT)
        return both[0:8] + both[8:16] + dot(rh, low_ref[...], NT)

    def coarse_correction():
        for q in range(4):
            hi, lo = v_hi[8 * q : 8 * q + 8, :], v_lo[8 * q : 8 * q + 8, :]
            rows = [slice(c * ROWS + 8 * q, c * ROWS + 8 * q + 8) for c in range(3)]
            got = pick(
                lambda c, r: wf[c * FROWS + r : c * FROWS + r + 1, :], FROWS, hi, lo,
                [wi[at, :] for at in rows],
            )
            for c in range(3):
                wi[rows[c], :] = got[c]
        for c in range(3):
            for r in range(ROWS):
                flat[c : c + 1, 128 * r : 128 * r + 128] = wi[c * ROWS + r : c * ROWS + r + 1, :]
        window = restricted(flat[...], pwh, pwl)
        for c in range(3):
            s1_send[:, WIN * c : WIN * c + WIN] = window[c : c + 1]
        s1_send[:, 3 * WIN :] = jnp.zeros((1, 256 - 3 * WIN), F32)
        s1_recv[d] = s1_send[...]
        lane = lax.broadcasted_iota(I32, (n_dev, 128), 1)
        first_at = 6 * lax.broadcasted_iota(I32, (n_dev, 128), 0) + (96 * g - 128 * block0)

        def to_all(src, dst, send_sems, recv_sems, along_dev, cover=None):
            me, count = (d, n_dev) if along_dev else (g, n_grp)
            copies = []
            for k in range(1, count):
                peer = lax.rem(me + k, count)
                copy = pltpu.make_async_remote_copy(
                    src_ref=src(peer),
                    dst_ref=dst.at[me],
                    send_sem=send_sems.at[k],
                    recv_sem=recv_sems.at[k],
                    device_id=(g, peer) if along_dev else (peer, d),
                    device_id_type=MESH,
                )
                copy.start()
                copies.append(copy)
            if cover is not None:
                cover()
            for copy in copies:
                copy.wait()

        def split_factor():
            for copy in l_copies:
                copy.wait()
            for b in range(6):
                at = slice(128 * b, 128 * b + 128)
                lbh[:, at], lbl[:, at] = split(lblk[b])

        to_all(lambda peer: s1_send, s1_recv, s1_ss, s1_rs, True, split_factor)
        windows = s1_recv[:, 0, :]
        span = []
        for c in range(3):
            row = []
            for b in range(2):
                at = lane + 128 * b - first_at
                inside = (at >= 0) & (at < WIN)
                at = jnp.where(inside, at, 0) + WIN * (c % 2)
                values = lane_gather(windows[:, 128 * (c // 2) : 128 * (c // 2) + 128], at)
                row.append(jnp.sum(jnp.where(inside, values, 0.0), axis=0, keepdims=True))
            span.append(row)
        acc = jnp.zeros((RB, 128), F32)
        for c in range(3):
            for b in range(2):
                acc = acc + lblk[2 * c + b] * span[c][b]
        ah, al = split(acc)
        s2_send[...] = dot(jnp.ones((16, 256), BF16), jnp.concatenate([ah, al], axis=1), NT)[0:1]
        s2_recv[g] = s2_send[...]
        to_all(lambda peer: s2_send, s2_recv, s2_ss, s2_rs, False)
        halfway = jnp.sum(s2_recv[:, 0, :], axis=0, keepdims=True)
        hh, hl = split(jnp.broadcast_to(halfway, (8, RB)))
        both = dot(jnp.concatenate([hh, hl], axis=0), lbh[...], NN)
        partial = both[0:1] + both[8:9] + dot(hh, lbl[...], NN)[0:1]
        parts = []
        for c in range(3):
            at = jnp.where(lane < WIN, lane, lane - WIN) + first_at
            values = []
            for b in range(2):
                row = partial[:, 256 * c + 128 * b : 256 * c + 128 * b + 128]
                values.append(
                    lane_gather(jnp.broadcast_to(row, (n_dev, 128)), jnp.clip(at - 128 * b, 0, 127))
                )
            parts.append(jnp.where(at < 128, values[0], values[1]))
        s3_send[:, 0, 0:128] = jnp.where(lane < WIN, parts[0], parts[1])
        s3_send[:, 0, 128:256] = parts[2]
        s3_recv[d] = s3_send[d]
        to_all(lambda peer: s3_send.at[peer], s3_recv, s3_ss, s3_rs, True)
        total = jnp.sum(s3_recv[:, 0, :], axis=0, keepdims=True)
        correction = jnp.concatenate(
            [total[:, WIN * c : WIN * c + WIN] for c in range(3)] + [jnp.zeros((5, WIN), F32)], axis=0
        )
        ch, cl = split(correction)
        left = jnp.concatenate([ch, cl], axis=0)
        both = dot(left, pwh[...], NN)
        flat[...] = both[0:8] + both[8:16] + dot(ch, pwl[...], NN)
        for c in range(3):
            for r in range(ROWS):
                wi[c * ROWS + r : c * ROWS + r + 1, :] = flat[c : c + 1, 128 * r : 128 * r + 128]
        zi[...] = zi[...] + wi[...]
        for half in range(2):
            hi, lo = f_hi[8 * half : 8 * half + 8, :], f_lo[8 * half : 8 * half + 8, :]
            got = pick(
                lambda c, r: wi[c * ROWS + r : c * ROWS + r + 1, :], ROWS, hi, lo,
                [jnp.zeros((8, 128), F32)] * 3,
            )
            for c in range(3):
                at = slice(c * FROWS + 8 * half, c * FROWS + 8 * half + 8)
                zf[at, :] = zf[at, :] + got[c]
        gather_interior()
        gather_faces(0)

    def apply(k, carry):
        @pl.when(k == 0)
        def _():
            put_product(main_diag * coef)

        @pl.when(k > 0)
        def _():
            gh, gl = split(gath[...])
            both = dot(m_hl[...], gh, NN)
            product = both[0:96] + both[96:192] + dot(m_hl[0:96, :], gl, NN)
            put_product(product * coef)

        for at, part in zip(face_rows(8), scatter_faces(hot_d)):
            wf[at, :] = mf[at, :] * zf[at, :] + part

        @pl.when(k == 0)
        def _():
            pl.semaphore_wait(barrier, n_dev + n_grp - 2)

        far = send_faces(k, (2, 3))
        for at, part in zip(face_rows(0), scatter_faces(hot_g)):
            wf[at, :] = mf[at, :] * zf[at, :] + part
        near = send_faces(k, (0, 1))

        @pl.when(k == 0)
        def _():
            lax.fori_loop(0, NODES_PER, one_hot_interior, 0)

        wi[...] = mi[...] * zi[...] + scatter(ROWS)

        @pl.when(k == 0)
        def _():
            di[...] = DAMPING / wi[...]
            zi[...] = ri[...] * di[...]
            at_faces(ri, rf, 0.0)
            mh, ml = split(dot_exact(dot_exact(place, em_ref[...], NN), place, NT))
            m_hl[0:96, :] = mh
            m_hl[96:192, :] = ml

        @pl.when(k == 2)
        def _():
            wi[...] = ri[...] - wi[...]
            flat[...] = jnp.zeros((8, 4096), F32)
            make_interpolation()

        @pl.when((k != 0) & (k != 2))
        def _():
            zi[...] = zi[...] + (ri[...] - wi[...]) * di[...]

        @pl.when((k != 2) & (k != 4))
        def _():
            gather_interior()

        add_faces(k, (0, 1), near)
        step_faces(k, 0)

        @pl.when((k != 2) & (k != 4))
        def _():
            gather_faces(0)

        add_faces(k, (2, 3), far)
        step_faces(k, 8)

        @pl.when(k == 2)
        def _():
            wf[...] = rf[...] - wf[...]
            coarse_correction()

        @pl.when(k != 4)
        def _():
            gather_faces(8)

        return carry

    zf[...] = jnp.ones((3 * FROWS, 128), F32)
    zi[...] = jnp.ones((3 * ROWS, 128), F32)
    lax.fori_loop(0, 5, apply, 0)
    for q in range(4):
        hi, lo = v_hi[8 * q : 8 * q + 8, :], v_lo[8 * q : 8 * q + 8, :]
        rows = [slice(c * ROWS + 8 * q, c * ROWS + 8 * q + 8) for c in range(3)]
        got = pick(
            lambda c, r: zf[c * FROWS + r : c * FROWS + r + 1, :], FROWS, hi, lo,
            [zi[at, :] for at in rows],
        )
        for c in range(3):
            out_ref[rows[c], :] = got[c]


def solution(mesh):
    n_grp, n_dev = mesh.shape["grp"], mesh.shape["dev"]

    def local(rhs, nodes, coef, mass, faces, coarse, weights, matrix, chol):
        dma = pltpu.SemaphoreType.DMA

        def body(*refs):
            kernel(n_grp, n_dev, *refs)

        out = pl.pallas_call(
            body,
            name="two_level",
            out_shape=jax.ShapeDtypeStruct((96, 128), F32),
            in_specs=[pl.BlockSpec(memory_space=pltpu.HBM)] * 9,
            out_specs=pl.BlockSpec(memory_space=pltpu.VMEM),
            scratch_shapes=[
                *[pltpu.VMEM((3 * n, 128), F32) for n in (FROWS, ROWS) * 5],
                pltpu.VMEM((32, ELEM), I32),
                pltpu.VMEM((32, ELEM), I32),
                pltpu.VMEM((96, ELEM), F32),
                pltpu.VMEM((96, ELEM), F32),
                pltpu.VMEM((96, ELEM), F32),
                pltpu.VMEM((192, 96), BF16),
                pltpu.VMEM((NODES_PER * ELEM, 128), BF16),
                pltpu.VMEM((NODES_PER, 16, ELEM), BF16),
                pltpu.VMEM((NODES_PER, 16, ELEM), BF16),
                pltpu.VMEM((NODES_PER, ROWS, ELEM), BF16),
                pltpu.VMEM((16, 128), I32),
                pltpu.VMEM((16, 128), I32),
                pltpu.VMEM((32, 128), I32),
                pltpu.VMEM((32, 128), I32),
                pltpu.VMEM((32, 128), I32),
                pltpu.VMEM((WIN, 4096), BF16),
                pltpu.VMEM((WIN, 4096), BF16),
                pltpu.VMEM((RB, 768), BF16),
                pltpu.VMEM((RB, 768), BF16),
                pltpu.VMEM((8, 4096), F32),
                pltpu.VMEM((27, 4, 128), I32),
                pltpu.VMEM((1, ELEM), F32),
                pltpu.VMEM((4, 512), I32),
                pltpu.VMEM((4, 4096), I32),
                pltpu.VMEM((4, 4096), F32),
                pltpu.VMEM((81, 81), F32),
                pltpu.VMEM((5, 4, 3, 4, 128), F32),
                pltpu.VMEM((5, 4, 3, 4, 128), F32),
                pltpu.VMEM((1, 256), F32),
                pltpu.VMEM((n_dev, 1, 256), F32),
                pltpu.VMEM((1, RB), F32),
                pltpu.VMEM((n_grp, 1, RB), F32),
                pltpu.VMEM((n_dev, 1, 256), F32),
                pltpu.VMEM((n_dev, 1, 256), F32),
                pltpu.VMEM((6, RB, 128), F32),
                dma((5, 4)), dma((5, 4)),
                dma((n_dev,)), dma((n_dev,)),
                dma((n_grp,)), dma((n_grp,)),
                dma((n_dev,)), dma((n_dev,)),
                dma((6,)),
                dma((8,)),
            ],
            compiler_params=pltpu.CompilerParams(
                collective_id=0, has_side_effects=True, vmem_limit_bytes=67_000_000
            ),
        )(
            rhs.reshape(96, 128), nodes.reshape(27, 4, 128), coef[0], mass.reshape(96, 128),
            faces[0, 0], coarse[0, 0], weights[0, 0], matrix, chol,
        )
        return out.reshape(1, 1, 3, 4096)

    return jax.shard_map(
        local,
        mesh=mesh,
        in_specs=(
            P("grp", "dev", None, None),
            P("grp", "dev", None, None),
            P("grp", "dev", None),
            P("grp", "dev", None, None),
            P("grp", "dev", None, None),
            P("grp", "dev", None, None),
            P("grp", "dev", None, None),
            P(),
            P("dev", None),
        ),
        out_specs=P("grp", "dev", None, None),
        check_vma=False,
    )
```

```python
import jax
import jax.numpy as jnp
from jax import lax
from jax.experimental import pallas as pl
from jax.experimental.pallas import tpu as pltpu
from jax.sharding import PartitionSpec as P

DAMPING = 0.6
MESH = pl.DeviceIdType.MESH
BF16 = jnp.bfloat16
F32 = jnp.float32
I32 = jnp.int32
NT = (((1,), (1,)), ((), ()))
NN = (((1,), (0,)), ((), ()))

ROWS = 32
FROWS = 16
NODES_PER = 27
ELEM = 512
CN = 1536
WIN = 64
RB = 288


def dot(a, b, dims):
    return lax.dot_general(a, b, dims, preferred_element_type=F32)


def dot_exact(a, b, dims):
    return lax.dot_general(
        a, b, dims, precision=lax.Precision.HIGHEST, preferred_element_type=F32
    )


def split(x):
    high = x.astype(BF16)
    low = (x - high.astype(F32)).astype(BF16)
    return high, low


def lane_gather(row, lanes):
    return jnp.take_along_axis(row, lanes, axis=1, mode="promise_in_bounds")


def pick(load_row, rows, hi, lo, start):
    got = list(start)
    fields = len(got)
    for r in range(rows):
        here = hi == r
        for c in range(fields):
            row = jnp.broadcast_to(load_row(c, r), hi.shape)
            got[c] = jnp.where(here, lane_gather(row, lo), got[c])
    return got


def kernel(
    n_grp, n_dev,
    rhs_hbm, nodes_hbm, coef_hbm, mass_hbm, face_hbm, cn_hbm, cw_hbm, em_hbm, chol_ref,
    out_ref,
    zf, zi, wf, wi, rf, ri, mf, mi, df, di,
    hi_i, lo_i, gath, p_hi, p_lo, m_hl, bn, oh,
    f_hi, f_lo, v_hi, v_lo, inv_t, pwh, pwl, lbh, lbl, flat,
    nodes_ref, coef_ref, face_ref, cn_ref, cw_ref, em_ref,
    send, recv, s1_send, s1_recv, s2_send, s2_recv, s3_send, s3_recv, lblk,
    send_sem, recv_sem, s1_ss, s1_rs, s2_ss, s2_rs, s3_ss, s3_rs, l_sem, in_sem,
):
    g = lax.axis_index("grp")
    d = lax.axis_index("dev")

    pairs = (
        (nodes_hbm, nodes_ref), (face_hbm, face_ref), (em_hbm, em_ref), (coef_hbm, coef_ref),
        (mass_hbm, mi), (rhs_hbm, ri), (cn_hbm, cn_ref), (cw_hbm, cw_ref),
    )
    loads = [pltpu.make_async_copy(a, b, in_sem.at[j]) for j, (a, b) in enumerate(pairs)]
    for load in loads:
        load.start()

    block0 = (3 * g) // 4
    block1 = lax.rem(block0 + 1, CN // 128)
    l_copies = []
    for c in range(3):
        for b, block in enumerate((block0, block1)):
            at = pl.multiple_of(CN * c + 128 * block, 128)
            copy = pltpu.make_async_copy(
                chol_ref.at[:, pl.ds(at, 128)], lblk.at[2 * c + b], l_sem.at[2 * c + b]
            )
            copy.start()
            l_copies.append(copy)

    barrier = pltpu.get_barrier_semaphore()
    for k in range(1, n_dev):
        pl.semaphore_signal(
            barrier, inc=1, device_id=(g, lax.rem(d + k, n_dev)), device_id_type=MESH
        )
    for k in range(1, n_grp):
        pl.semaphore_signal(
            barrier, inc=1, device_id=(lax.rem(g + k, n_grp), d), device_id_type=MESH
        )

    for load in loads:
        load.wait()
    for f in range(4):
        for r in range(4):
            face = face_ref[f : f + 1, 128 * r : 128 * r + 128]
            f_hi[4 * f + r : 4 * f + r + 1, :] = face >> 7
            f_lo[4 * f + r : 4 * f + r + 1, :] = face & 127

    def one_hot(index_row, count):
        at = jnp.broadcast_to(index_row, (count, index_row.shape[1]))
        number = lax.broadcasted_iota(I32, at.shape, 0)
        return jnp.where(at == number, 1.0, 0.0).astype(BF16)

    acc = jnp.zeros((64, 128), F32)
    for f in range(4):
        face = face_ref[f : f + 1, :]
        hot = one_hot(face >> 7, ROWS)
        slot = lax.broadcasted_iota(I32, (ROWS, ELEM), 1) + (512 * f + 1)
        a = jnp.concatenate(
            [(slot >> 6).astype(F32).astype(BF16) * hot, (slot & 63).astype(F32).astype(BF16) * hot],
            axis=0,
        )
        acc = acc + dot(a, one_hot(face & 127, 128), NT)
    inverse = (64.0 * acc[0:32] + acc[32:64]).astype(I32) - 1
    inv_t[...] = inverse
    v_hi[...] = inverse >> 7
    v_lo[...] = inverse & 127

    hi_i[...] = jnp.zeros((32, ELEM), I32)
    lo_i[...] = jnp.zeros((32, ELEM), I32)
    for i in range(NODES_PER):
        for k in range(4):
            index = nodes_ref[i, k : k + 1, :]
            hi_i[i : i + 1, 128 * k : 128 * k + 128] = index >> 7
            lo_i[i : i + 1, 128 * k : 128 * k + 128] = index & 127

    def renumber(v, carry):
        row = pl.multiple_of(8 * (v // 4), 8)
        lane = pl.multiple_of(128 * (v % 4), 128)
        at = (pl.ds(row, 8), pl.ds(lane, 128))
        hi, lo = hi_i[at], lo_i[at]
        slot = pick(lambda c, r: inv_t[r : r + 1, :], ROWS, hi, lo, [jnp.full((8, 128), -1, I32)])[0]
        hi_i[at] = jnp.where(slot >= 0, slot >> 7, hi + FROWS)
        lo_i[at] = jnp.where(slot >= 0, slot & 127, lo)
        return carry

    lax.fori_loop(0, 16, renumber, 0, unroll=4)

    def one_hot_faces(i, carry):
        oh[i, 0:FROWS] = one_hot(hi_i[pl.ds(i, 1), :], FROWS)
        return carry

    def one_hot_interior(i, carry):
        oh[i, FROWS:] = one_hot(hi_i[pl.ds(i, 1), :] - FROWS, ROWS)
        return carry

    lax.fori_loop(0, NODES_PER, one_hot_faces, 0)
    turned = lo_i[...].astype(F32).T
    number = lax.broadcasted_iota(I32, (ELEM, 128), 1).astype(F32)
    for i in range(NODES_PER):
        same = jnp.broadcast_to(turned[:, i : i + 1], (ELEM, 128)) == number
        bn[ELEM * i : ELEM * i + ELEM, :] = jnp.where(same, 1.0, 0.0).astype(BF16)

    def at_faces(source, target, idle):
        for half in range(2):
            hi, lo = f_hi[8 * half : 8 * half + 8, :], f_lo[8 * half : 8 * half + 8, :]
            got = pick(
                lambda c, r: source[c * ROWS + r : c * ROWS + r + 1, :], ROWS, hi, lo,
                [jnp.full((8, 128), idle, F32)] * 3,
            )
            for c in range(3):
                target[c * FROWS + 8 * half : c * FROWS + 8 * half + 8, :] = got[c]

    at_faces(mi, mf, 1.0)

    row_of = lax.broadcasted_iota(I32, (96, 81), 0)
    col_of = lax.broadcasted_iota(I32, (96, 81), 1)
    place = (col_of == 27 * (row_of // 32) + row_of % 32) & (row_of % 32 < 27)
    place = jnp.where(place, 1.0, 0.0)
    eye = lax.broadcasted_iota(I32, (81, 81), 0) == lax.broadcasted_iota(I32, (81, 81), 1)
    diag_row = jnp.sum(jnp.where(eye, em_ref[...], 0.0), axis=0, keepdims=True)
    main_diag = jnp.sum(place * diag_row, axis=1, keepdims=True)
    coef = coef_ref[...]

    def put_product(product):
        high = product.astype(BF16).astype(F32)
        p_hi[...] = high
        p_lo[...] = product - high

    def scatter(first, rows):
        columns = []
        for i in range(NODES_PER):
            hot = oh[i, first : first + rows]
            blocks = []
            for part in (p_hi, p_lo):
                for c in range(3):
                    row = part[c * 32 + i : c * 32 + i + 1, :]
                    value = jnp.broadcast_to(row, (rows, ELEM)).astype(BF16)
                    blocks.append(value * hot)
            columns.append(jnp.concatenate(blocks, axis=0))
        acc = dot(jnp.concatenate(columns, axis=1), bn[...], NN)
        return acc[0 : 3 * rows] + acc[3 * rows : 6 * rows]

    up_g, down_g = lax.rem(g + 1, n_grp), lax.rem(g + n_grp - 1, n_grp)
    up_d, down_d = lax.rem(d + 1, n_dev), lax.rem(d + n_dev - 1, n_dev)
    partners = ((down_g, d), (up_g, d), (g, down_d), (g, up_d))

    def send_faces(k):
        for f in (2, 3, 0, 1):
            for c in range(3):
                send[k, f, c] = wf[c * FROWS + 4 * f : c * FROWS + 4 * f + 4, :]
        copies = []
        for f in (2, 3, 0, 1):
            copy = pltpu.make_async_remote_copy(
                src_ref=send.at[k, f],
                dst_ref=recv.at[k, f ^ 1],
                send_sem=send_sem.at[k, f],
                recv_sem=recv_sem.at[k, f ^ 1],
                device_id=partners[f],
                device_id_type=MESH,
            )
            copy.start()
            copies.append(copy)
        return copies

    def add_faces(k, faces, copies):
        for copy in copies:
            copy.wait()
        for f in faces:
            for c in range(3):
                at = slice(c * FROWS + 4 * f, c * FROWS + 4 * f + 4)
                wf[at, :] = wf[at, :] + recv[k, f, c]

    def gather(table, stride, base, first, rows, fresh, unroll):
        def body(v, carry):
            row = pl.multiple_of(8 * (v // 4), 8)
            lane = pl.multiple_of(128 * (v % 4), 128)
            hi, lo = hi_i[pl.ds(row, 8), pl.ds(lane, 128)], lo_i[pl.ds(row, 8), pl.ds(lane, 128)]
            if fresh:
                start = [jnp.zeros((8, 128), F32)] * 3
            else:
                start = [gath[pl.ds(row + 32 * c, 8), pl.ds(lane, 128)] for c in range(3)]
            got = pick(
                lambda c, r: table[c * stride + base + r : c * stride + base + r + 1, :],
                rows, hi - first, lo, start,
            )
            for c in range(3):
                gath[pl.ds(row + 32 * c, 8), pl.ds(lane, 128)] = got[c]
            return carry

        lax.fori_loop(0, 16, body, 0, unroll=unroll)

    def gather_interior():
        gather(zi, ROWS, 0, FROWS, ROWS, True, 8)

    def gather_faces(base):
        gather(zf, FROWS, base, base, 8, False, 8)

    def face_rows(base):
        return [slice(c * FROWS + base, c * FROWS + base + 8) for c in range(3)]

    def step_faces(k, base):
        @pl.when(k == 0)
        def _():
            for at in face_rows(base):
                df[at, :] = DAMPING / wf[at, :]
                zf[at, :] = rf[at, :] * df[at, :]

        @pl.when((k != 0) & (k != 2))
        def _():
            for at in face_rows(base):
                zf[at, :] = zf[at, :] + (rf[at, :] - wf[at, :]) * df[at, :]

    home = 6 * (n_dev * g + d)

    def fill(high_ref, low_ref, at, nodes, weights):
        shape = (WIN, nodes[0].shape[1])
        number = lax.broadcasted_iota(I32, shape, 0)
        total = jnp.zeros(shape, F32)
        for node, weight in zip(nodes, weights):
            rel = node - home
            rel = jnp.where(rel < 0, rel + CN, rel)
            hit = jnp.broadcast_to(rel, shape) == number
            total = total + jnp.where(hit, jnp.broadcast_to(weight, shape), 0.0)
        high_ref[:, at], low_ref[:, at] = split(total)

    def make_interpolation():
        def body(q, carry):
            at = pl.ds(pl.multiple_of(512 * q, 512), 512)
            fill(
                pwh, pwl, at,
                [cn_ref[j : j + 1, at] for j in range(4)], [cw_ref[j : j + 1, at] for j in range(4)],
            )
            return carry

        lax.fori_loop(0, 8, body, 0)

    def restricted(values, high_ref, low_ref):
        rh, rl = split(values)
        both = dot(jnp.concatenate([rh, rl], axis=0), high_ref[...], NT)
        return both[0:8] + both[8:16] + dot(rh, low_ref[...], NT)

    def coarse_correction():
        for q in range(4):
            hi, lo = v_hi[8 * q : 8 * q + 8, :], v_lo[8 * q : 8 * q + 8, :]
            rows = [slice(c * ROWS + 8 * q, c * ROWS + 8 * q + 8) for c in range(3)]
            got = pick(
                lambda c, r: wf[c * FROWS + r : c * FROWS + r + 1, :], FROWS, hi, lo,
                [wi[at, :] for at in rows],
            )
            for c in range(3):
                wi[rows[c], :] = got[c]
        for c in range(3):
            for r in range(ROWS):
                flat[c : c + 1, 128 * r : 128 * r + 128] = wi[c * ROWS + r : c * ROWS + r + 1, :]
        window = restricted(flat[...], pwh, pwl)
        for c in range(3):
            s1_send[:, WIN * c : WIN * c + WIN] = window[c : c + 1]
        s1_send[:, 3 * WIN :] = jnp.zeros((1, 256 - 3 * WIN), F32)
        s1_recv[d] = s1_send[...]
        lane = lax.broadcasted_iota(I32, (n_dev, 128), 1)
        first_at = 6 * lax.broadcasted_iota(I32, (n_dev, 128), 0) + (96 * g - 128 * block0)

        def to_all(src, dst, send_sems, recv_sems, along_dev, cover=None):
            me, count = (d, n_dev) if along_dev else (g, n_grp)
            copies = []
            for k in range(1, count):
                peer = lax.rem(me + k, count)
                copy = pltpu.make_async_remote_copy(
                    src_ref=src(peer),
                    dst_ref=dst.at[me],
                    send_sem=send_sems.at[k],
                    recv_sem=recv_sems.at[k],
                    device_id=(g, peer) if along_dev else (peer, d),
                    device_id_type=MESH,
                )
                copy.start()
                copies.append(copy)
            if cover is not None:
                cover()
            for copy in copies:
                copy.wait()

        def split_factor():
            for copy in l_copies:
                copy.wait()
            for b in range(6):
                at = slice(128 * b, 128 * b + 128)
                lbh[:, at], lbl[:, at] = split(lblk[b])

        to_all(lambda peer: s1_send, s1_recv, s1_ss, s1_rs, True, split_factor)
        windows = s1_recv[:, 0, :]
        span = []
        for c in range(3):
            row = []
            for b in range(2):
                at = lane + 128 * b - first_at
                inside = (at >= 0) & (at < WIN)
                at = jnp.where(inside, at, 0) + WIN * (c % 2)
                values = lane_gather(windows[:, 128 * (c // 2) : 128 * (c // 2) + 128], at)
                row.append(jnp.sum(jnp.where(inside, values, 0.0), axis=0, keepdims=True))
            span.append(row)
        acc = jnp.zeros((RB, 128), F32)
        for c in range(3):
            for b in range(2):
                acc = acc + lblk[2 * c + b] * span[c][b]
        ah, al = split(acc)
        s2_send[...] = dot(jnp.ones((16, 256), BF16), jnp.concatenate([ah, al], axis=1), NT)[0:1]
        s2_recv[g] = s2_send[...]
        to_all(lambda peer: s2_send, s2_recv, s2_ss, s2_rs, False)
        halfway = jnp.sum(s2_recv[:, 0, :], axis=0, keepdims=True)
        hh, hl = split(jnp.broadcast_to(halfway, (8, RB)))
        both = dot(jnp.concatenate([hh, hl], axis=0), lbh[...], NN)
        partial = both[0:1] + both[8:9] + dot(hh, lbl[...], NN)[0:1]
        parts = []
        for c in range(3):
            at = jnp.where(lane < WIN, lane, lane - WIN) + first_at
            values = []
            for b in range(2):
                row = partial[:, 256 * c + 128 * b : 256 * c + 128 * b + 128]
                values.append(
                    lane_gather(jnp.broadcast_to(row, (n_dev, 128)), jnp.clip(at - 128 * b, 0, 127))
                )
            parts.append(jnp.where(at < 128, values[0], values[1]))
        s3_send[:, 0, 0:128] = jnp.where(lane < WIN, parts[0], parts[1])
        s3_send[:, 0, 128:256] = parts[2]
        s3_recv[d] = s3_send[d]
        to_all(lambda peer: s3_send.at[peer], s3_recv, s3_ss, s3_rs, True)
        total = jnp.sum(s3_recv[:, 0, :], axis=0, keepdims=True)
        correction = jnp.concatenate(
            [total[:, WIN * c : WIN * c + WIN] for c in range(3)] + [jnp.zeros((5, WIN), F32)], axis=0
        )
        ch, cl = split(correction)
        left = jnp.concatenate([ch, cl], axis=0)
        both = dot(left, pwh[...], NN)
        flat[...] = both[0:8] + both[8:16] + dot(ch, pwl[...], NN)
        for c in range(3):
            for r in range(ROWS):
                wi[c * ROWS + r : c * ROWS + r + 1, :] = flat[c : c + 1, 128 * r : 128 * r + 128]
        zi[...] = zi[...] + wi[...]
        for half in range(2):
            hi, lo = f_hi[8 * half : 8 * half + 8, :], f_lo[8 * half : 8 * half + 8, :]
            got = pick(
                lambda c, r: wi[c * ROWS + r : c * ROWS + r + 1, :], ROWS, hi, lo,
                [jnp.zeros((8, 128), F32)] * 3,
            )
            for c in range(3):
                at = slice(c * FROWS + 8 * half, c * FROWS + 8 * half + 8)
                zf[at, :] = zf[at, :] + got[c]
        gather_interior()
        gather_faces(0)

    def apply(k, carry):
        @pl.when(k == 0)
        def _():
            put_product(main_diag * coef)

        @pl.when(k > 0)
        def _():
            gh, gl = split(gath[...])
            both = dot(m_hl[...], gh, NN)
            product = both[0:96] + both[96:192] + dot(m_hl[0:96, :], gl, NN)
            put_product(product * coef)

        wf[...] = mf[...] * zf[...] + scatter(0, FROWS)

        @pl.when(k == 0)
        def _():
            pl.semaphore_wait(barrier, n_dev + n_grp - 2)

        copies = send_faces(k)

        @pl.when(k == 0)
        def _():
            lax.fori_loop(0, NODES_PER, one_hot_interior, 0)

        wi[...] = mi[...] * zi[...] + scatter(FROWS, ROWS)

        @pl.when(k == 0)
        def _():
            di[...] = DAMPING / wi[...]
            zi[...] = ri[...] * di[...]
            at_faces(ri, rf, 0.0)
            mh, ml = split(dot_exact(dot_exact(place, em_ref[...], NN), place, NT))
            m_hl[0:96, :] = mh
            m_hl[96:192, :] = ml

        @pl.when(k == 2)
        def _():
            wi[...] = ri[...] - wi[...]
            flat[...] = jnp.zeros((8, 4096), F32)
            make_interpolation()

        @pl.when((k != 0) & (k != 2))
        def _():
            zi[...] = zi[...] + (ri[...] - wi[...]) * di[...]

        @pl.when((k != 2) & (k != 4))
        def _():
            gather_interior()

        add_faces(k, (0, 1), copies[2:])
        step_faces(k, 0)

        @pl.when((k != 2) & (k != 4))
        def _():
            gather_faces(0)

        add_faces(k, (2, 3), copies[:2])
        step_faces(k, 8)

        @pl.when(k == 2)
        def _():
            wf[...] = rf[...] - wf[...]
            coarse_correction()

        @pl.when(k != 4)
        def _():
            gather_faces(8)

        return carry

    zf[...] = jnp.ones((3 * FROWS, 128), F32)
    zi[...] = jnp.ones((3 * ROWS, 128), F32)
    lax.fori_loop(0, 5, apply, 0)
    for q in range(4):
        hi, lo = v_hi[8 * q : 8 * q + 8, :], v_lo[8 * q : 8 * q + 8, :]
        rows = [slice(c * ROWS + 8 * q, c * ROWS + 8 * q + 8) for c in range(3)]
        got = pick(
            lambda c, r: zf[c * FROWS + r : c * FROWS + r + 1, :], FROWS, hi, lo,
            [zi[at, :] for at in rows],
        )
        for c in range(3):
            out_ref[rows[c], :] = got[c]


def solution(mesh):
    n_grp, n_dev = mesh.shape["grp"], mesh.shape["dev"]

    def local(rhs, nodes, coef, mass, faces, coarse, weights, matrix, chol):
        dma = pltpu.SemaphoreType.DMA

        def body(*refs):
            kernel(n_grp, n_dev, *refs)

        out = pl.pallas_call(
            body,
            name="two_level",
            out_shape=jax.ShapeDtypeStruct((96, 128), F32),
            in_specs=[pl.BlockSpec(memory_space=pltpu.HBM)] * 9,
            out_specs=pl.BlockSpec(memory_space=pltpu.VMEM),
            scratch_shapes=[
                *[pltpu.VMEM((3 * n, 128), F32) for n in (FROWS, ROWS) * 5],
                pltpu.VMEM((32, ELEM), I32),
                pltpu.VMEM((32, ELEM), I32),
                pltpu.VMEM((96, ELEM), F32),
                pltpu.VMEM((96, ELEM), F32),
                pltpu.VMEM((96, ELEM), F32),
                pltpu.VMEM((192, 96), BF16),
                pltpu.VMEM((NODES_PER * ELEM, 128), BF16),
                pltpu.VMEM((NODES_PER, FROWS + ROWS, ELEM), BF16),
                pltpu.VMEM((16, 128), I32),
                pltpu.VMEM((16, 128), I32),
                pltpu.VMEM((32, 128), I32),
                pltpu.VMEM((32, 128), I32),
                pltpu.VMEM((32, 128), I32),
                pltpu.VMEM((WIN, 4096), BF16),
                pltpu.VMEM((WIN, 4096), BF16),
                pltpu.VMEM((RB, 768), BF16),
                pltpu.VMEM((RB, 768), BF16),
                pltpu.VMEM((8, 4096), F32),
                pltpu.VMEM((27, 4, 128), I32),
                pltpu.VMEM((1, ELEM), F32),
                pltpu.VMEM((4, 512), I32),
                pltpu.VMEM((4, 4096), I32),
                pltpu.VMEM((4, 4096), F32),
                pltpu.VMEM((81, 81), F32),
                pltpu.VMEM((5, 4, 3, 4, 128), F32),
                pltpu.VMEM((5, 4, 3, 4, 128), F32),
                pltpu.VMEM((1, 256), F32),
                pltpu.VMEM((n_dev, 1, 256), F32),
                pltpu.VMEM((1, RB), F32),
                pltpu.VMEM((n_grp, 1, RB), F32),
                pltpu.VMEM((n_dev, 1, 256), F32),
                pltpu.VMEM((n_dev, 1, 256), F32),
                pltpu.VMEM((6, RB, 128), F32),
                dma((5, 4)), dma((5, 4)),
                dma((n_dev,)), dma((n_dev,)),
                dma((n_grp,)), dma((n_grp,)),
                dma((n_dev,)), dma((n_dev,)),
                dma((6,)),
                dma((8,)),
            ],
            compiler_params=pltpu.CompilerParams(
                collective_id=0, has_side_effects=True, vmem_limit_bytes=67_000_000
            ),
        )(
            rhs.reshape(96, 128), nodes.reshape(27, 4, 128), coef[0], mass.reshape(96, 128),
            faces[0, 0], coarse[0, 0], weights[0, 0], matrix, chol,
        )
        return out.reshape(1, 1, 3, 4096)

    return jax.shard_map(
        local,
        mesh=mesh,
        in_specs=(
            P("grp", "dev", None, None),
            P("grp", "dev", None, None),
            P("grp", "dev", None),
            P("grp", "dev", None, None),
            P("grp", "dev", None, None),
            P("grp", "dev", None, None),
            P("grp", "dev", None, None),
            P(),
            P("dev", None),
        ),
        out_specs=P("grp", "dev", None, None),
        check_vma=False,
    )
```
